32 devices in a mesh: dp: 8 (over z, core), space: 4 (over y, x).
Axes of the slice: x: 2, y: 2, z: 4, core: 2. Of those that a mesh axis runs over, the one named last changes fastest.
Arguments:
- inputs: bfloat16 [8, 24, 32, 32, 256], P('dp', 'space'), may hold values from -6 to 6
- kernels: bfloat16 [2, 3, 3, 256, 256], P(None, None, None, 'dp'), may hold values from -0.125 to 0.125
- cotangent: bfloat16 [8, 24, 32, 32, 256], P('dp', 'space'), may hold values from -0.01171875 to 0.01171875
- adjacency: int32 [24, 4, 3], P('space'), may hold values from 0 to 23, as said below
Outputs:
- final_state: bfloat16 [8, 24, 32, 32, 256], P('dp', 'space')
- kernel_grads: float32 [2, 3, 3, 256, 256], P(None, None, None, 'dp')
The draws below stay inside these ranges and needn't reach their ends.
Inputs may be any that keep to these rules, and one draw needn't show every extreme that they name: Entry [t, e] = (n, f, r): edge e of tile t meets edge f of tile n, and r = 1 where the two edges are read in opposite directions along the shared line. The relation is symmetric: adjacency[n, f] = (t, e, r). The tiles form 2 x 2 blocks on the six faces of a cube, numbered in an order drawn from the seed.
All inputs are finite; a program needn't handle non-finite values.
Results may differ from the reference program's by a relative error of at most 0.005.
Values may be sent and summed in bfloat16 or wider, within the bound.
A program may use at most 192 MiB of HBM per device.

```python
import jax
import jax.numpy as jnp
import numpy as np

C = 256
S = 32
FACE_SPLIT = 2
LAYERS = 2
TILES = 24
BATCH = 8


def vector_cross(first, second):
    return np.array([int(first[1]) * int(second[2]) - int(first[2]) * int(second[1]), int(first[2]) * int(second[0]) - int(first[0]) * int(second[2]), int(first[0]) * int(second[1]) - int(first[1]) * int(second[0])], np.int64)


def same_vector(first, second):
    return all((int(first[index]) == int(second[index]) for index in range(3)))


def edge_dirs(frame):
    normal, tangent_a, tangent_b = frame
    return [(-tangent_a, tangent_b), (tangent_a, tangent_b), (-tangent_b, tangent_a), (tangent_b, tangent_a)]


def cube_tables(split_num):
    frames = []
    for axis_num in range(3):
        for sign_val in (1, -1):
            normal = np.zeros(3, np.int64)
            normal[axis_num] = sign_val
            tangent_a = np.zeros(3, np.int64)
            tangent_a[(axis_num + 1) % 3] = 1
            tangent_b = vector_cross(normal, tangent_a)
            frames.append((normal, tangent_a, tangent_b))
    centers = {}
    for face_num in range(6):
        normal, tangent_a, tangent_b = frames[face_num]
        for row_num in range(split_num):
            for col_num in range(split_num):
                center_pt = split_num * normal + (2 * row_num + 1 - split_num) * tangent_a + (2 * col_num + 1 - split_num) * tangent_b
                centers[tuple((int(entry) for entry in center_pt))] = face_num * split_num * split_num + row_num * split_num + col_num
    tile_count = 6 * split_num * split_num
    neighbor = np.zeros((tile_count, 4), np.int64)
    facing = np.zeros((tile_count, 4), np.int64)
    reversal = np.zeros((tile_count, 4), np.int64)
    for face_num in range(6):
        normal, tangent_a, tangent_b = frames[face_num]
        directions = edge_dirs(frames[face_num])
        for row_num in range(split_num):
            for col_num in range(split_num):
                position = face_num * split_num * split_num + row_num * split_num + col_num
                center_pt = split_num * normal + (2 * row_num + 1 - split_num) * tangent_a + (2 * col_num + 1 - split_num) * tangent_b
                for edge_num in range(4):
                    outward, along_dir = directions[edge_num]
                    step_row = row_num + (-1 if edge_num == 0 else 1 if edge_num == 1 else 0)
                    step_col = col_num + (-1 if edge_num == 2 else 1 if edge_num == 3 else 0)
                    if 0 <= step_row < split_num and 0 <= step_col < split_num:
                        neighbor[position, edge_num] = face_num * split_num * split_num + step_row * split_num + step_col
                        facing[position, edge_num] = edge_num ^ 1
                        reversal[position, edge_num] = 0
                    else:
                        across_pt = center_pt + outward - normal
                        across = centers[tuple((int(entry) for entry in across_pt))]
                        across_face = across // (split_num * split_num)
                        across_dirs = edge_dirs(frames[across_face])
                        back_edge = [candidate for candidate in range(4) if same_vector(across_dirs[candidate][0], -normal)][0]
                        neighbor[position, edge_num] = across
                        facing[position, edge_num] = back_edge
                        reversal[position, edge_num] = 0 if same_vector(across_dirs[back_edge][1], along_dir) else 1
    return np.stack([neighbor, facing, reversal], axis=2)


def draw_adjacency(key, part):
    table = jnp.asarray(cube_tables(FACE_SPLIT), jnp.int32)
    shuffled = jax.random.permutation(key, 6 * FACE_SPLIT * FACE_SPLIT).astype(jnp.int32)
    positions = jnp.argsort(shuffled).astype(jnp.int32)
    rows_here = table[positions]
    return jnp.stack([shuffled[rows_here[:, :, 0]], rows_here[:, :, 1], rows_here[:, :, 2]], axis=2).astype(jnp.int32)


def shard_levels(stream_key, shape, shards, least, largest):
    def one(dim, shards_of):
        steps = jax.random.uniform(jax.random.fold_in(jax.random.fold_in(stream_key, 6), dim), (shards_of,), jnp.float32, least / len(shards), largest / len(shards))
        return jnp.repeat(jnp.exp(steps), shape[dim] // shards_of).reshape((-1,) + (1,) * (len(shape) - dim - 1))

    level = one(*shards[0])
    for cut in shards[1:]:
        level = level * one(*cut)
    return level


def centred(rng, dims, deviation, reach, shards=(), held_as=jnp.bfloat16):
    factor_of = shard_levels(rng, dims, shards, -0.22, 0.18) if shards else 1.0
    entries = jax.random.normal(rng, dims, jnp.float32) * deviation * factor_of
    return jnp.minimum(jnp.maximum(entries, -reach), reach).astype(held_as)


def setup_inputs(seed: int = 0) -> dict:
    seeds = jax.random.split(jax.random.key(seed), 5)
    inputs = centred(seeds[0], (BATCH, TILES, S, S, C), 1.0, 6.0, ((0, 8), (1, 4)))
    kernels = centred(seeds[1], (LAYERS, 3, 3, C, C), (9 * C) ** -0.5, 0.125, ((3, 8),))
    cotangent = centred(seeds[2], (BATCH, TILES, S, S, C), 0.002, 0.01171875, ((0, 8), (1, 4)))
    adjacency = draw_adjacency(jax.random.fold_in(seeds[4], 71), 0)
    return {"inputs": inputs, "kernels": kernels, "cotangent": cotangent, "adjacency": adjacency}


def edge_strips(tile_field):
    return jnp.stack([tile_field[:, :, 0], tile_field[:, :, -1], tile_field[:, :, :, 0], tile_field[:, :, :, -1]], axis=2)

def orient(strips, adjacency):
    selected = strips[:, adjacency[:, :, 0], adjacency[:, :, 1]]
    flipped = (adjacency[:, :, 2] == 1)[None, :, :, None, None]
    return jnp.where(flipped, selected[:, :, :, ::-1], selected)

def with_rim(tile_field, rim_rows):
    padded = jnp.pad(tile_field, ((0, 0), (0, 0), (1, 1), (1, 1), (0, 0)))
    padded = padded.at[:, :, 0, 1:-1].set(rim_rows[:, :, 0])
    padded = padded.at[:, :, -1, 1:-1].set(rim_rows[:, :, 1])
    padded = padded.at[:, :, 1:-1, 0].set(rim_rows[:, :, 2])
    padded = padded.at[:, :, 1:-1, -1].set(rim_rows[:, :, 3])
    return padded

def convolve(padded, kernel):
    extent = padded.shape[2] - 2
    channels = padded.shape[-1]
    summed = jnp.zeros(padded.shape[:2] + (extent, extent, kernel.shape[-1]), jnp.float32)
    for row_off in range(3):
        for col_off in range(3):
            patches = padded[:, :, row_off:row_off + extent, col_off:col_off + extent].reshape(-1, channels)
            summed = summed + jnp.dot(patches, kernel[row_off, col_off], preferred_element_type=jnp.float32).reshape(summed.shape)
    return summed

def weight_grad(padded, flat_grad):
    extent = padded.shape[2] - 2
    channels = padded.shape[-1]
    rows_out = []
    for row_off in range(3):
        row_list = []
        for col_off in range(3):
            patches = padded[:, :, row_off:row_off + extent, col_off:col_off + extent].reshape(-1, channels)
            row_list.append(jnp.dot(patches.T, flat_grad, preferred_element_type=jnp.float32))
        rows_out.append(jnp.stack(row_list))
    return jnp.stack(rows_out)

def input_grad(flat_grad, kernel, padded_shape):
    extent = padded_shape[2] - 2
    pad_grad = jnp.zeros(padded_shape, jnp.float32)
    piece_shape = padded_shape[:2] + (extent, extent, padded_shape[4])
    for row_off in range(3):
        for col_off in range(3):
            contrib = jnp.dot(flat_grad, kernel[row_off, col_off].T, preferred_element_type=jnp.float32).reshape(piece_shape)
            pad_grad = pad_grad.at[:, :, row_off:row_off + extent, col_off:col_off + extent].add(contrib)
    return pad_grad

def rim_strips(pad_grad):
    return jnp.stack([pad_grad[:, :, 0, 1:-1], pad_grad[:, :, -1, 1:-1], pad_grad[:, :, 1:-1, 0], pad_grad[:, :, 1:-1, -1]], axis=2)

def add_rim(interior, returned):
    interior = interior.at[:, :, 0].add(returned[:, :, 0])
    interior = interior.at[:, :, -1].add(returned[:, :, 1])
    interior = interior.at[:, :, :, 0].add(returned[:, :, 2])
    interior = interior.at[:, :, :, -1].add(returned[:, :, 3])
    return interior

def reference(inputs, kernels, cotangent, adjacency):
    current = inputs
    stored = []
    for layer_num in range(LAYERS):
        rim_rows = orient(edge_strips(current), adjacency)
        padded = with_rim(current, rim_rows)
        preact = convolve(padded, kernels[layer_num])
        current = (current.astype(jnp.float32) + jax.nn.silu(preact)).astype(jnp.bfloat16)
        stored.append((padded, preact))
    upstream = cotangent.astype(jnp.float32)
    kernel_grads = [None] * LAYERS
    for layer_num in range(LAYERS - 1, -1, -1):
        padded, preact = stored[layer_num]
        logistic = jax.nn.sigmoid(preact)
        pre_grad = (upstream * logistic * (1.0 + preact * (1.0 - logistic))).astype(jnp.bfloat16)
        flat_grad = pre_grad.reshape(-1, pre_grad.shape[-1])
        kernel_grads[layer_num] = weight_grad(padded, flat_grad)
        if layer_num > 0:
            pad_grad = input_grad(flat_grad, kernels[layer_num], padded.shape)
            rim_values = rim_strips(pad_grad).astype(jnp.bfloat16)
            returned = orient(rim_values, adjacency).astype(jnp.float32)
            upstream = add_rim(upstream + pad_grad[:, :, 1:-1, 1:-1], returned)
    return (current, jnp.stack(kernel_grads))
```

```python
import functools

import jax
import jax.numpy as jnp
from jax import lax
from jax.experimental import pallas as pl
from jax.experimental.pallas import tpu as pltpu
from jax.sharding import PartitionSpec as P

LAYERS = 2
F32 = jnp.float32
BF16 = jnp.bfloat16


def edge_strips(field):
    return jnp.stack(
        [field[:, 0], field[:, -1], field[:, :, 0], field[:, :, -1]], axis=1
    )


def orient(strips, adjacency):
    selected = strips[adjacency[:, :, 0], adjacency[:, :, 1]]
    flipped = (adjacency[:, :, 2] == 1)[:, :, None, None]
    return jnp.where(flipped, selected[:, :, ::-1], selected)


def exchange(strips, adjacency):
    return orient(lax.all_gather(strips, "space", axis=0, tiled=True), adjacency)


def fill(x3, field, rims):
    s, _, c = field.shape
    col = lax.broadcasted_iota(jnp.int32, (s, s, c), 1)
    wide = field.astype(F32)
    if rims is None:
        left = right = jnp.zeros((1, 1, 1), F32)
    else:
        left = rims[2].astype(F32)[:, None, :]
        right = rims[3].astype(F32)[:, None, :]
    x3[1 : s + 1, :, c : 2 * c] = field
    x3[1 : s + 1, :, 0:c] = jnp.where(col == 0, left, pltpu.roll(wide, 1, 1)).astype(BF16)
    x3[1 : s + 1, :, 2 * c :] = jnp.where(
        col == s - 1, right, pltpu.roll(wide, s - 1, 1)
    ).astype(BF16)
    rc = lax.broadcasted_iota(jnp.int32, (s, c), 0)
    for row, edge in ((0, 0), (s + 1, 1)):
        if rims is None:
            x3[row] = jnp.zeros((s, 3 * c), BF16)
        else:
            line = rims[edge].astype(F32)
            x3[row, :, c : 2 * c] = rims[edge]
            x3[row, :, 0:c] = jnp.where(rc == 0, 0.0, pltpu.roll(line, 1, 0)).astype(BF16)
            x3[row, :, 2 * c :] = jnp.where(
                rc == s - 1, 0.0, pltpu.roll(line, s - 1, 0)
            ).astype(BF16)


def conv(x3, w):
    s = x3.shape[1]
    k = x3.shape[2]
    total = None
    for p in range(3):
        part = jnp.dot(
            x3[p : p + s].reshape(s * s, k), w[p], preferred_element_type=F32
        )
        total = part if total is None else total + part
    return total.reshape(s, s, -1)


def wgrad_add(acc, x3, grad):
    s = x3.shape[1]
    k = x3.shape[2]
    flipped = grad.reshape(s * s, -1).T
    for p in range(3):
        acc[p] += jnp.dot(
            flipped, x3[p : p + s].reshape(s * s, k), preferred_element_type=F32
        )


def k_first(x, rims, w, state, slope, x3):
    fill(x3, x[0], rims[0])
    v = conv(x3, w)
    sg = jax.nn.sigmoid(v)
    state[0] = (x[0].astype(F32) + v * sg).astype(BF16)
    slope[0] = (sg * (1.0 + v * (1.0 - sg))).astype(slope.dtype)


def k_last(x, rims, w, wt, cot, state, grad, rim_grad, x3, g3):
    s = x.shape[1]
    c = x.shape[3]
    fill(x3, x[0], rims[0])
    v = conv(x3, w)
    sg = jax.nn.sigmoid(v)
    state[0] = (x[0].astype(F32) + v * sg).astype(BF16)
    g32 = cot[0].astype(F32) * (sg * (1.0 + v * (1.0 - sg)))
    g = g32.astype(BF16)
    grad[0] = g
    fill(g3, g, None)
    rim_grad[0, 0] = jnp.dot(g3[1], wt[2], preferred_element_type=F32).astype(BF16)
    rim_grad[0, 1] = jnp.dot(g3[s], wt[0], preferred_element_type=F32).astype(BF16)
    for edge, col, q in ((2, 0, 2), (3, s - 1, 0)):
        line = jnp.concatenate(
            [g3[p : p + s, :, c : 2 * c].astype(F32)[:, col, :] for p in range(3)], axis=1
        ).astype(BF16)
        weight = jnp.concatenate([wt[p, q * c : (q + 1) * c] for p in range(3)], axis=0)
        rim_grad[0, edge] = jnp.dot(line, weight, preferred_element_type=F32).astype(BF16)


def finish_wgrad(acc, out):
    @pl.when(pl.program_id(0) == pl.num_programs(0) - 1)
    def _():
        for p in range(3):
            out[p] = acc[p].T


def k_back(x, rims, g, wt, cot, up, dw, x3, g3, acc):
    @pl.when(pl.program_id(0) == 0)
    def _():
        acc[...] = jnp.zeros_like(acc)

    fill(x3, x[0], rims[0])
    wgrad_add(acc, x3, g[0])
    fill(g3, g[0], None)
    up[0] = cot[0].astype(F32) + conv(g3, wt)
    finish_wgrad(acc, dw)


def k_tail(x, rims, up, back, slope, dw, x3, acc):
    @pl.when(pl.program_id(0) == 0)
    def _():
        acc[...] = jnp.zeros_like(acc)

    s = x.shape[1]
    fill(x3, x[0], rims[0])
    u = up[0]
    row = lax.broadcasted_iota(jnp.int32, u.shape, 0)
    col = lax.broadcasted_iota(jnp.int32, u.shape, 1)
    r = back[0].astype(F32)
    u = u + jnp.where(row == 0, r[0][None], 0.0) + jnp.where(row == s - 1, r[1][None], 0.0)
    u = u + jnp.where(col == 0, r[2][:, None, :], 0.0)
    u = u + jnp.where(col == s - 1, r[3][:, None, :], 0.0)
    g = (u * slope[0].astype(F32)).astype(BF16)
    wgrad_add(acc, x3, g)
    finish_wgrad(acc, dw)


def reduce_grad(dw, c):
    dw = dw.reshape(3, 3, c, c)
    part = lax.psum_scatter(dw, "dp", scatter_dimension=2, tiled=True)
    return lax.psum(part, "space")


def per_device(inputs, kernels, cotangent, adjacency):
    _, t, s, _, c = inputs.shape
    x0 = inputs[0]
    cot = cotangent[0]
    weights = [lax.all_gather(kernels[l], "dp", axis=2, tiled=True) for l in range(2)]
    w1 = weights[0].reshape(3, 3 * c, c)
    w2 = weights[1].reshape(3, 3 * c, c)
    wt = jnp.transpose(weights[1][::-1, ::-1], (0, 1, 3, 2)).reshape(3, 3 * c, c)

    tile = pl.BlockSpec((1, s, s, c), lambda i: (i, 0, 0, 0))
    rim = pl.BlockSpec((1, 4, s, c), lambda i: (i, 0, 0, 0))
    wsp = pl.BlockSpec((3, 3 * c, c), lambda i: (0, 0, 0), pipeline_mode=pl.Buffered(1))
    field = lambda dt: jax.ShapeDtypeStruct((t, s, s, c), dt)
    dws = jax.ShapeDtypeStruct((3, 3 * c, c), F32)
    x3s = pltpu.VMEM((s + 2, s, 3 * c), BF16)
    accs = pltpu.VMEM((3, c, 3 * c), F32)
    flops = 2 * t * s * s * c * c * 9
    call = lambda body, nf, ins, outs, shapes, scratch: pl.pallas_call(
        body,
        grid=(t,),
        in_specs=ins,
        out_specs=outs,
        out_shape=shapes,
        scratch_shapes=scratch,
        compiler_params=pltpu.CompilerParams(vmem_limit_bytes=60 << 20),
        cost_estimate=pl.CostEstimate(
            flops=nf * flops, bytes_accessed=12 << 20, transcendentals=0
        ),
    )
    rims0 = exchange(edge_strips(x0), adjacency)
    state1, slope1 = call(
        k_first, 1, [tile, rim, wsp], [tile, tile], [field(BF16), field(BF16)], [x3s]
    )(x0, rims0, w1)
    rims1 = exchange(edge_strips(state1), adjacency)
    state2, g2, rg = call(
        k_last,
        1,
        [tile, rim, wsp, wsp, tile],
        [tile, tile, rim],
        [field(BF16), field(BF16), jax.ShapeDtypeStruct((t, 4, s, c), BF16)],
        [x3s, x3s],
    )(state1, rims1, w2, wt, cot)
    back = exchange(rg, adjacency)
    up, dw2 = call(
        k_back, 2, [tile, rim, tile, wsp, tile], [tile, wsp], [field(F32), dws], [x3s, x3s, accs]
    )(state1, rims1, g2, wt, cot)
    dw2r = reduce_grad(dw2, c)
    dw1 = call(k_tail, 1, [tile, rim, tile, rim, tile], wsp, dws, [x3s, accs])(
        x0, rims0, up, back, slope1
    )
    dw1r = reduce_grad(dw1, c)
    return state2[None], jnp.stack([dw1r, dw2r])


def solution(mesh):
    in_specs = (
        P("dp", "space", None, None, None),
        P(None, None, None, "dp", None),
        P("dp", "space", None, None, None),
        P("space", None, None),
    )
    out_specs = (P("dp", "space", None, None, None), P(None, None, None, "dp", None))
    return jax.shard_map(
        per_device, mesh=mesh, in_specs=in_specs, out_specs=out_specs, check_vma=False
    )
```

```python
import functools

import jax
import jax.numpy as jnp
from jax import lax
from jax.experimental import pallas as pl
from jax.experimental.pallas import tpu as pltpu
from jax.sharding import PartitionSpec as P

LAYERS = 2
F32 = jnp.float32
BF16 = jnp.bfloat16


def edge_strips(field):
    return jnp.stack(
        [field[:, 0], field[:, -1], field[:, :, 0], field[:, :, -1]], axis=1
    )


def orient(strips, adjacency):
    selected = strips[adjacency[:, :, 0], adjacency[:, :, 1]]
    flipped = (adjacency[:, :, 2] == 1)[:, :, None, None]
    return jnp.where(flipped, selected[:, :, ::-1], selected)


def exchange(strips, adjacency, n_sp, cid):
    if n_sp == 4:
        every = swap_strips(strips, cid).reshape((-1,) + strips.shape[1:])
    else:
        every = lax.all_gather(strips, "space", axis=0, tiled=True)
    return orient(every, adjacency)


def fill(x3, field, rims):
    s, _, c = field.shape
    col = lax.broadcasted_iota(jnp.int32, (s, s, c), 1)
    wide = field.astype(F32)
    if rims is None:
        left = right = jnp.zeros((1, 1, 1), F32)
    else:
        left = rims[2].astype(F32)[:, None, :]
        right = rims[3].astype(F32)[:, None, :]
    x3[1 : s + 1, :, c : 2 * c] = field
    x3[1 : s + 1, :, 0:c] = jnp.where(col == 0, left, pltpu.roll(wide, 1, 1)).astype(BF16)
    x3[1 : s + 1, :, 2 * c :] = jnp.where(
        col == s - 1, right, pltpu.roll(wide, s - 1, 1)
    ).astype(BF16)
    rc = lax.broadcasted_iota(jnp.int32, (s, c), 0)
    for row, edge in ((0, 0), (s + 1, 1)):
        if rims is None:
            x3[row] = jnp.zeros((s, 3 * c), BF16)
        else:
            line = rims[edge].astype(F32)
            x3[row, :, c : 2 * c] = rims[edge]
            x3[row, :, 0:c] = jnp.where(rc == 0, 0.0, pltpu.roll(line, 1, 0)).astype(BF16)
            x3[row, :, 2 * c :] = jnp.where(
                rc == s - 1, 0.0, pltpu.roll(line, s - 1, 0)
            ).astype(BF16)


def conv(x3, w):
    s = x3.shape[1]
    k = x3.shape[2]
    total = None
    for p in range(3):
        part = jnp.dot(
            x3[p : p + s].reshape(s * s, k), w[p], preferred_element_type=F32
        )
        total = part if total is None else total + part
    return total.reshape(s, s, -1)


def wgrad_add(acc, x3, grad):
    s = x3.shape[1]
    k = x3.shape[2]
    flipped = grad.reshape(s * s, -1).T
    for p in range(3):
        acc[p] += jnp.dot(
            flipped, x3[p : p + s].reshape(s * s, k), preferred_element_type=F32
        )


def k_first(x, rims, w, state, slope, x3):
    fill(x3, x[0], rims[0])
    v = conv(x3, w)
    sg = jax.nn.sigmoid(v)
    state[0] = (x[0].astype(F32) + v * sg).astype(BF16)
    slope[0] = (sg * (1.0 + v * (1.0 - sg))).astype(slope.dtype)


def k_last(x, rims, w, wt, cot, state, grad, rim_grad, x3, g3):
    s = x.shape[1]
    c = x.shape[3]
    fill(x3, x[0], rims[0])
    v = conv(x3, w)
    sg = jax.nn.sigmoid(v)
    state[0] = (x[0].astype(F32) + v * sg).astype(BF16)
    g32 = cot[0].astype(F32) * (sg * (1.0 + v * (1.0 - sg)))
    g = g32.astype(BF16)
    grad[0] = g
    fill(g3, g, None)
    rim_grad[0, 0] = jnp.dot(g3[1], wt[2], preferred_element_type=F32).astype(BF16)
    rim_grad[0, 1] = jnp.dot(g3[s], wt[0], preferred_element_type=F32).astype(BF16)
    for edge, col, q in ((2, 0, 2), (3, s - 1, 0)):
        line = jnp.concatenate(
            [g3[p : p + s, :, c : 2 * c].astype(F32)[:, col, :] for p in range(3)], axis=1
        ).astype(BF16)
        weight = jnp.concatenate([wt[p, q * c : (q + 1) * c] for p in range(3)], axis=0)
        rim_grad[0, edge] = jnp.dot(line, weight, preferred_element_type=F32).astype(BF16)


def finish_wgrad(acc, out):
    @pl.when(pl.program_id(0) == pl.num_programs(0) - 1)
    def _():
        n, _, c = out.shape
        depth = c // n
        for p in range(3):
            for q in range(3):
                tap = acc[p, :, q * c : (q + 1) * c].T.astype(out.dtype)
                first = (3 * p + q) * depth
                out[:, first : first + depth, :] = tap.reshape(n, depth, c)


def k_back(x, rims, g, wt, cot, up, dw, x3, g3, acc):
    @pl.when(pl.program_id(0) == 0)
    def _():
        acc[...] = jnp.zeros_like(acc)

    fill(x3, x[0], rims[0])
    wgrad_add(acc, x3, g[0])
    fill(g3, g[0], None)
    up[0] = cot[0].astype(F32) + conv(g3, wt)
    finish_wgrad(acc, dw)


def k_tail(x, rims, up, back, slope, dw, x3, acc):
    @pl.when(pl.program_id(0) == 0)
    def _():
        acc[...] = jnp.zeros_like(acc)

    s = x.shape[1]
    fill(x3, x[0], rims[0])
    u = up[0]
    row = lax.broadcasted_iota(jnp.int32, u.shape, 0)
    col = lax.broadcasted_iota(jnp.int32, u.shape, 1)
    r = back[0].astype(F32)
    u = u + jnp.where(row == 0, r[0][None], 0.0) + jnp.where(row == s - 1, r[1][None], 0.0)
    u = u + jnp.where(col == 0, r[2][:, None, :], 0.0)
    u = u + jnp.where(col == s - 1, r[3][:, None, :], 0.0)
    g = (u * slope[0].astype(F32)).astype(BF16)
    wgrad_add(acc, x3, g)
    finish_wgrad(acc, dw)


def reduce_grads(dw1, dw2, n_dp, n_sp):
    both = jnp.concatenate([dw1, dw2], axis=1)
    n, rows, c = both.shape
    if n_sp == 4:
        total = sum_grads(n_dp, both, 3)
    else:
        part = lax.psum_scatter(both.astype(F32), "dp", scatter_dimension=0, tiled=True)
        total = lax.psum(part, "space")
    return total.reshape(LAYERS, 3, 3, c // n, c)


def remote(src, dst, sems, i, who):
    return pltpu.make_async_remote_copy(
        src_ref=src,
        dst_ref=dst,
        send_sem=sems.at[0, i],
        recv_sem=sems.at[1, i],
        device_id=who,
        device_id_type=pl.DeviceIdType.MESH,
    )


def square():
    me = lax.axis_index("space")
    xn = me + 1 - 2 * (me % 2)
    yn = (me + 2) % 4
    return me, xn, yn, (xn + 2) % 4


def swap_start(src, out, sems):
    me, xn, yn, _ = square()
    h = src.shape[0] // 2
    lo, hi = pl.ds(0, h), pl.ds(h, src.shape[0] - h)
    copies = [
        remote(src.at[lo], out.at[me, lo], sems, 0, {"space": xn}),
        remote(src.at[hi], out.at[me, hi], sems, 1, {"space": yn}),
        remote(src.at[hi], out.at[me, hi], sems, 2, {"space": xn}),
        remote(src.at[lo], out.at[me, lo], sems, 3, {"space": yn}),
    ]
    for copy in copies:
        copy.start()
    return copies


def swap_relay(copies, out, sems):
    me, xn, yn, _ = square()
    t = out.shape[1]
    h = t // 2
    lo, hi = pl.ds(0, h), pl.ds(h, t - h)
    copies[0].wait_recv()
    first = remote(out.at[xn, lo], out.at[xn, lo], sems, 4, {"space": yn})
    first.start()
    copies[1].wait_recv()
    second = remote(out.at[yn, hi], out.at[yn, hi], sems, 5, {"space": xn})
    second.start()
    return copies + [first, second]


def swap_end(copies):
    for i, copy in enumerate(copies):
        copy.wait_send()
        if i >= 2:
            copy.wait_recv()


def greet(peers):
    barrier = pltpu.get_barrier_semaphore()
    for who in peers:
        pl.semaphore_signal(
            barrier, inc=1, device_id=who, device_id_type=pl.DeviceIdType.MESH
        )
    pl.semaphore_wait(barrier, len(peers))


def c_swap(src, out, sems, own):
    me, xn, yn, _ = square()
    greet([{"space": xn}, {"space": yn}])
    copies = swap_start(src, out, sems)
    local = pltpu.make_async_copy(src, out.at[me], own)
    local.start()
    swap_end(swap_relay(copies, out, sems))
    local.wait()


def c_open(n_dp, w_in, src, w_out, out, sems, own, zs, ps):
    me, xn, yn, _ = square()
    line = n_dp // 2
    dp = lax.axis_index("dp")
    q, core = dp // 2, dp % 2
    depth = w_in.shape[3]
    layers = w_in.shape[0]
    right = {"dp": ((q + 1) % line) * 2 + core}
    left = {"dp": ((q + line - 1) % line) * 2 + core}
    partner = {"dp": q * 2 + 1 - core}
    greet([{"space": xn}, {"space": yn}, right, left, partner])
    copies = swap_start(src, out, sems)
    local = pltpu.make_async_copy(src, out.at[me], own.at[0])
    local.start()

    def slot(l, o, c):
        return w_out.at[l, :, :, pl.ds(pl.multiple_of((o * 2 + c) * depth, depth), depth), :]

    keep = pltpu.make_async_copy(
        w_in, w_out.at[:, :, :, pl.ds(pl.multiple_of(dp * depth, depth), depth), :], own.at[1]
    )
    keep.start()

    def move(l, o, who, sm, i, first):
        ref = w_in.at[l] if first else slot(l, o, core)
        return remote(ref, slot(l, o, core), sm, i, who)

    def zi(l, s, way):
        return (l * line + s) * 2 + way

    def forward(l, s, way, o, first):
        who = right if way == 0 else left
        ok = (q + 1 < line) if way == 0 else (q > 0)

        @pl.when(ok)
        def _():
            move(l, o, who, zs, zi(l, s, way), first).start()

    for l in range(layers):
        forward(l, 0, 0, q, True)
        forward(l, 0, 1, q, True)
        move(l, q, partner, ps, zi(l, 0, 0), True).start()
    copies = swap_relay(copies, out, sems)
    for l in range(layers):
        for s in range(1, line):
            for way in (0, 1):
                o = q - s if way == 0 else q + s
                ok = (o >= 0) if way == 0 else (o < line)

                @pl.when(ok)
                def _(l=l, s=s, way=way, o=o):
                    move(l, o, right, zs, zi(l, s - 1, way), False).wait_recv()
                    move(l, o, partner, ps, zi(l, s, way), False).start()
                    if s < line - 1:
                        forward(l, s, way, o, False)

    for l in range(layers):
        for s in range(line):
            for way in (0, 1):
                o = q - s if way == 0 else q + s
                ok = (o >= 0) if way == 0 else (o < line)
                if s == 0 and way == 1:
                    ok = None

                def part(l=l, s=s, way=way, o=o):
                    copy = move(l, o, partner, ps, zi(l, s, way), False)
                    copy.wait_send()
                    remote(
                        slot(l, o, 1 - core), slot(l, o, 1 - core), ps, zi(l, s, way), partner
                    ).wait_recv()

                if ok is not None:
                    pl.when(ok)(part)
                if s < line - 1:
                    sent = (
                        jnp.logical_and(o >= 0, q + 1 < line)
                        if way == 0
                        else jnp.logical_and(o < line, q > 0)
                    )

                    @pl.when(sent)
                    def _(l=l, s=s, way=way, o=o):
                        move(l, o, right, zs, zi(l, s, way), False).wait_send()

    swap_end(copies)
    local.wait()
    keep.wait()


def c_sum(n_dp, g, out, b1, x_out, x_in, keep2, y_out, y_in, keep3, z_out, z_in, a_out, a_in, sems):
    me, xn, yn, _ = square()
    line = n_dp // 2
    dp = lax.axis_index("dp")
    q, core = dp // 2, dp % 2
    rows = g.shape[2]
    rh = rows // 2
    ry = y_in.shape[1]
    partner = {"dp": q * 2 + 1 - core}
    zp = [{"dp": ((q + d) % line) * 2 + core} for d in range(1, line)]
    mx, my = me % 2, me // 2
    x_mine = pl.multiple_of(mx * rh, 16)
    x_give = pl.multiple_of((1 - mx) * rh, 16)
    y_mine = pl.multiple_of(my * (rh - ry), 16)
    y_give = pl.multiple_of((1 - my) * (rh - ry), 16)
    greet([{"space": xn}, {"space": yn}, partner] + zp)
    give = remote(g.at[:, 1 - core, pl.ds(x_give, rh)], b1.at[:, pl.ds(x_give, rh)], sems, 0, partner)
    give.start()
    have = remote(g.at[:, 1 - core, pl.ds(x_mine, rh)], b1.at[:, pl.ds(x_mine, rh)], sems, 1, partner)
    have.start()
    give.wait_recv()
    for l in range(line):
        x_out[l] = (
            g[l, core, pl.ds(x_give, rh)].astype(F32) + b1[l, pl.ds(x_give, rh)].astype(F32)
        ).astype(BF16)
    sx = remote(x_out, x_in, sems, 2, {"space": xn})
    sx.start()
    have.wait_recv()
    for l in range(line):
        keep2[l] = g[l, core, pl.ds(x_mine, rh)].astype(F32) + b1[l, pl.ds(x_mine, rh)].astype(F32)
    sx.wait_recv()
    for l in range(line):
        y_out[l] = (
            keep2[l, pl.ds(y_give, ry)] + x_in[l, pl.ds(y_give, ry)].astype(F32)
        ).astype(BF16)
    sy = remote(y_out, y_in, sems, 3, {"space": yn})
    sy.start()
    for l in range(line):
        keep3[l] = keep2[l, pl.ds(y_mine, ry)] + x_in[l, pl.ds(y_mine, ry)].astype(F32)
    sy.wait_recv()
    for l in range(line):
        keep3[l] = keep3[l] + y_in[l].astype(F32)
    z_out[...] = keep3[...].astype(BF16)
    moves = []
    for d in range(1, line):
        copy = remote(z_out.at[(q + d) % line], z_in.at[d - 1], sems, 3 + d, zp[d - 1])
        copy.start()
        moves.append(copy)
    total = keep3[q]
    for d, copy in enumerate(moves):
        copy.wait_recv()
        total = total + z_in[d].astype(F32)
    a_out[...] = total.astype(BF16)
    back = pl.multiple_of(x_mine + y_mine, 16)
    fy = remote(a_out, a_in.at[0, pl.ds(0, ry)], sems, 3 + line, {"space": yn})
    fy.start()
    fx = remote(a_out, a_in.at[1, pl.ds(0, ry)], sems, 4 + line, {"space": xn})
    fx.start()
    fy.wait_recv()
    fz = remote(a_in.at[0, pl.ds(0, ry)], a_in.at[2, pl.ds(0, ry)], sems, 5 + line, {"space": xn})
    fz.start()
    out[pl.ds(back, ry)] = a_out[...].astype(F32)
    out[pl.ds(pl.multiple_of(x_mine + y_give, 16), ry)] = a_in[0].astype(F32)
    fx.wait_recv()
    out[pl.ds(pl.multiple_of(x_give + y_mine, 16), ry)] = a_in[1].astype(F32)
    fz.wait_recv()
    out[pl.ds(pl.multiple_of(x_give + y_give, 16), ry)] = a_in[2].astype(F32)
    for copy in [give, have, sx, sy, fy, fx, fz] + moves:
        copy.wait_send()


VM = pl.BlockSpec(memory_space=pltpu.VMEM)


def params(cid):
    return pltpu.CompilerParams(
        collective_id=cid, has_side_effects=True, vmem_limit_bytes=60 << 20
    )


def swap_strips(strips, cid):
    dma = pltpu.SemaphoreType.DMA
    return pl.pallas_call(
        c_swap,
        out_shape=jax.ShapeDtypeStruct((4,) + strips.shape, strips.dtype),
        in_specs=[VM],
        out_specs=VM,
        scratch_shapes=[dma((2, 6)), dma],
        compiler_params=params(cid),
    )(strips)


def open_gather(n_dp, kernels, strips):
    dma = pltpu.SemaphoreType.DMA
    shape = kernels.shape
    whole = shape[:3] + (shape[3] * n_dp, shape[4])
    return pl.pallas_call(
        functools.partial(c_open, n_dp),
        out_shape=(
            jax.ShapeDtypeStruct(whole, kernels.dtype),
            jax.ShapeDtypeStruct((4,) + strips.shape, strips.dtype),
        ),
        in_specs=[VM, VM],
        out_specs=(VM, VM),
        scratch_shapes=[
            dma((2, 6)),
            dma((2,)),
            dma((2, 2 * n_dp)),
            dma((2, 2 * n_dp)),
        ],
        compiler_params=params(0),
    )(kernels, strips)


def sum_grads(n_dp, g, cid):
    line = n_dp // 2
    rows, c = g.shape[1:]
    g = g.reshape(line, 2, rows, c)
    rh = rows // 2
    ry = -(-(rh // 2) // 16) * 16
    vm = pltpu.VMEM
    return pl.pallas_call(
        functools.partial(c_sum, n_dp),
        out_shape=jax.ShapeDtypeStruct((rows, c), F32),
        in_specs=[VM],
        out_specs=VM,
        scratch_shapes=[
            vm((line, rows, c), BF16),
            vm((line, rh, c), BF16),
            vm((line, rh, c), BF16),
            vm((line, rh, c), F32),
            vm((line, ry, c), BF16),
            vm((line, ry, c), BF16),
            vm((line, ry, c), F32),
            vm((line, ry, c), BF16),
            vm((line - 1, ry, c), BF16),
            vm((ry, c), BF16),
            vm((3, ry, c), BF16),
            pltpu.SemaphoreType.DMA((2, 6 + line)),
        ],
        compiler_params=params(cid),
    )(g)


def per_device(n_dp, n_sp, inputs, kernels, cotangent, adjacency):
    _, t, s, _, c = inputs.shape
    x0 = inputs[0]
    cot = cotangent[0]
    if n_sp == 4:
        weights, every = open_gather(n_dp, kernels, edge_strips(x0))
        rims0 = orient(every.reshape((-1, 4, s, c)), adjacency)
    else:
        weights = lax.all_gather(kernels, "dp", axis=3, tiled=True)
        rims0 = exchange(edge_strips(x0), adjacency, n_sp, 0)
    w1 = weights[0].reshape(3, 3 * c, c)
    w2 = weights[1].reshape(3, 3 * c, c)
    wt = jnp.transpose(weights[1][::-1, ::-1], (0, 1, 3, 2)).reshape(3, 3 * c, c)

    tile = pl.BlockSpec((1, s, s, c), lambda i: (i, 0, 0, 0))
    rim = pl.BlockSpec((1, 4, s, c), lambda i: (i, 0, 0, 0))
    wsp = pl.BlockSpec((3, 3 * c, c), lambda i: (0, 0, 0), pipeline_mode=pl.Buffered(1))
    field = lambda dt: jax.ShapeDtypeStruct((t, s, s, c), dt)
    dws = jax.ShapeDtypeStruct((n_dp, 9 * c // n_dp, c), BF16)
    dwsp = pl.BlockSpec(dws.shape, lambda i: (0, 0, 0))
    x3s = pltpu.VMEM((s + 2, s, 3 * c), BF16)
    accs = pltpu.VMEM((3, c, 3 * c), F32)
    flops = 2 * t * s * s * c * c * 9
    call = lambda body, nf, ins, outs, shapes, scratch: pl.pallas_call(
        body,
        grid=(t,),
        in_specs=ins,
        out_specs=outs,
        out_shape=shapes,
        scratch_shapes=scratch,
        compiler_params=pltpu.CompilerParams(vmem_limit_bytes=60 << 20),
        cost_estimate=pl.CostEstimate(
            flops=nf * flops, bytes_accessed=12 << 20, transcendentals=0
        ),
    )
    state1, slope1 = call(
        k_first, 1, [tile, rim, wsp], [tile, tile], [field(BF16), field(F32)], [x3s]
    )(x0, rims0, w1)
    rims1 = exchange(edge_strips(state1), adjacency, n_sp, 1)
    state2, g2, rg = call(
        k_last,
        1,
        [tile, rim, wsp, wsp, tile],
        [tile, tile, rim],
        [field(BF16), field(BF16), jax.ShapeDtypeStruct((t, 4, s, c), BF16)],
        [x3s, x3s],
    )(state1, rims1, w2, wt, cot)
    back = exchange(rg, adjacency, n_sp, 2)
    up, dw2 = call(
        k_back, 2, [tile, rim, tile, wsp, tile], [tile, dwsp], [field(F32), dws], [x3s, x3s, accs]
    )(state1, rims1, g2, wt, cot)
    dw1 = call(k_tail, 1, [tile, rim, tile, rim, tile], dwsp, dws, [x3s, accs])(
        x0, rims0, up, back, slope1
    )
    return state2[None], reduce_grads(dw1, dw2, n_dp, n_sp)


def solution(mesh):
    in_specs = (
        P("dp", "space", None, None, None),
        P(None, None, None, "dp", None),
        P("dp", "space", None, None, None),
        P("space", None, None),
    )
    out_specs = (P("dp", "space", None, None, None), P(None, None, None, "dp", None))
    body = functools.partial(per_device, mesh.shape["dp"], mesh.shape["space"])
    return jax.shard_map(
        body, mesh=mesh, in_specs=in_specs, out_specs=out_specs, check_vma=False
    )
```

```python
import functools

import jax
import jax.numpy as jnp
from jax import lax
from jax.experimental import pallas as pl
from jax.experimental.pallas import tpu as pltpu
from jax.sharding import PartitionSpec as P

LAYERS = 2
F32 = jnp.float32
BF16 = jnp.bfloat16


def edge_strips(field):
    return jnp.stack(
        [field[:, 0], field[:, -1], field[:, :, 0], field[:, :, -1]], axis=1
    )


def orient(strips, adjacency):
    selected = strips[adjacency[:, :, 0], adjacency[:, :, 1]]
    flipped = (adjacency[:, :, 2] == 1)[:, :, None, None]
    return jnp.where(flipped, selected[:, :, ::-1], selected)


def exchange(strips, adjacency):
    return orient(lax.all_gather(strips, "space", axis=0, tiled=True), adjacency)


def fill(x3, field, rims):
    s, _, c = field.shape
    col = lax.broadcasted_iota(jnp.int32, (s, s, c), 1)
    wide = field.astype(F32)
    if rims is None:
        left = right = jnp.zeros((1, 1, 1), F32)
    else:
        left = rims[2].astype(F32)[:, None, :]
        right = rims[3].astype(F32)[:, None, :]
    x3[1 : s + 1, :, c : 2 * c] = field
    x3[1 : s + 1, :, 0:c] = jnp.where(col == 0, left, pltpu.roll(wide, 1, 1)).astype(BF16)
    x3[1 : s + 1, :, 2 * c :] = jnp.where(
        col == s - 1, right, pltpu.roll(wide, s - 1, 1)
    ).astype(BF16)
    rc = lax.broadcasted_iota(jnp.int32, (s, c), 0)
    for row, edge in ((0, 0), (s + 1, 1)):
        if rims is None:
            x3[row] = jnp.zeros((s, 3 * c), BF16)
        else:
            line = rims[edge].astype(F32)
            x3[row, :, c : 2 * c] = rims[edge]
            x3[row, :, 0:c] = jnp.where(rc == 0, 0.0, pltpu.roll(line, 1, 0)).astype(BF16)
            x3[row, :, 2 * c :] = jnp.where(
                rc == s - 1, 0.0, pltpu.roll(line, s - 1, 0)
            ).astype(BF16)


def conv(x3, w):
    s = x3.shape[1]
    k = x3.shape[2]
    total = None
    for p in range(3):
        part = jnp.dot(
            x3[p : p + s].reshape(s * s, k), w[p], preferred_element_type=F32
        )
        total = part if total is None else total + part
    return total.reshape(s, s, -1)


def wgrad_add(acc, x3, grad):
    s = x3.shape[1]
    k = x3.shape[2]
    flipped = grad.reshape(s * s, -1).T
    for p in range(3):
        acc[p] += jnp.dot(
            flipped, x3[p : p + s].reshape(s * s, k), preferred_element_type=F32
        )


def k_first_send(x, rims, w, adj, state, slope, rims_out, x3, gath, sems):
    stream_begin()
    t = rims_out.shape[0]
    out = k_first(x, rims, w, state, slope, x3)
    put_strips(gath, t, pl.program_id(0), out)
    stream_tile(gath, sems, t, adj, rims_out)


def k_first_only(*refs):
    k_first(*refs)


def k_last_send(x, rims, w, wt, cot, adj, state, grad, back, x3, g3, rim_grad, gath, sems):
    stream_begin()
    t = back.shape[0]
    k_last(x, rims, w, wt, cot, state, grad, rim_grad, x3, g3)
    me = lax.axis_index("space")
    base = (me * t + pl.program_id(0)) * 4
    for e in range(4):
        gath[base + e] = rim_grad[0, e]
    stream_tile(gath, sems, t, adj, back)


def k_first(x, rims, w, state, slope, x3):
    fill(x3, x[0], rims[0])
    v = conv(x3, w)
    sg = jax.nn.sigmoid(v)
    out = x[0].astype(F32) + v * sg
    state[0] = out.astype(BF16)
    slope[0] = (sg * (1.0 + v * (1.0 - sg))).astype(slope.dtype)
    return out


def k_last(x, rims, w, wt, cot, state, grad, rim_grad, x3, g3):
    s = x.shape[1]
    c = x.shape[3]
    fill(x3, x[0], rims[0])
    v = conv(x3, w)
    sg = jax.nn.sigmoid(v)
    state[0] = (x[0].astype(F32) + v * sg).astype(BF16)
    g32 = cot[0].astype(F32) * (sg * (1.0 + v * (1.0 - sg)))
    g = g32.astype(BF16)
    grad[0] = g
    fill(g3, g, None)
    rim_grad[0, 0] = jnp.dot(g3[1], wt[2], preferred_element_type=F32).astype(BF16)
    rim_grad[0, 1] = jnp.dot(g3[s], wt[0], preferred_element_type=F32).astype(BF16)
    for edge, col, q in ((2, 0, 2), (3, s - 1, 0)):
        line = jnp.concatenate(
            [g3[p : p + s, :, c : 2 * c].astype(F32)[:, col, :] for p in range(3)], axis=1
        ).astype(BF16)
        weight = jnp.concatenate([wt[p, q * c : (q + 1) * c] for p in range(3)], axis=0)
        rim_grad[0, edge] = jnp.dot(line, weight, preferred_element_type=F32).astype(BF16)


def finish_wgrad(acc, out):
    @pl.when(pl.program_id(0) == pl.num_programs(0) - 1)
    def _():
        n, _, c = out.shape
        depth = c // n
        for p in range(3):
            for q in range(3):
                tap = acc[p, :, q * c : (q + 1) * c].T.astype(out.dtype)
                first = (3 * p + q) * depth
                out[:, first : first + depth, :] = tap.reshape(n, depth, c)


def k_back(x, rims, g, wt, cot, up, dw, x3, g3, acc):
    @pl.when(pl.program_id(0) == 0)
    def _():
        acc[...] = jnp.zeros_like(acc)

    fill(x3, x[0], rims[0])
    wgrad_add(acc, x3, g[0])
    fill(g3, g[0], None)
    up[0] = cot[0].astype(F32) + conv(g3, wt)
    finish_wgrad(acc, dw)


def k_tail(x, rims, up, back, slope, dw, x3, acc):
    @pl.when(pl.program_id(0) == 0)
    def _():
        acc[...] = jnp.zeros_like(acc)

    s = x.shape[1]
    fill(x3, x[0], rims[0])
    u = up[0]
    row = lax.broadcasted_iota(jnp.int32, u.shape, 0)
    col = lax.broadcasted_iota(jnp.int32, u.shape, 1)
    r = back[0].astype(F32)
    u = u + jnp.where(row == 0, r[0][None], 0.0) + jnp.where(row == s - 1, r[1][None], 0.0)
    u = u + jnp.where(col == 0, r[2][:, None, :], 0.0)
    u = u + jnp.where(col == s - 1, r[3][:, None, :], 0.0)
    g = (u * slope[0].astype(F32)).astype(BF16)
    wgrad_add(acc, x3, g)
    finish_wgrad(acc, dw)


def reduce_grads(dw1, dw2, n_dp, n_sp):
    both = jnp.concatenate([dw1, dw2], axis=1)
    n, rows, c = both.shape
    if n_sp == 4:
        total = sum_grads(n_dp, both, 3)
    else:
        part = lax.psum_scatter(both.astype(F32), "dp", scatter_dimension=0, tiled=True)
        total = lax.psum(part, "space")
    return total.reshape(LAYERS, 3, 3, c // n, c)


def remote(src, dst, sems, i, who):
    return pltpu.make_async_remote_copy(
        src_ref=src,
        dst_ref=dst,
        send_sem=sems.at[0, i],
        recv_sem=sems.at[1, i],
        device_id=who,
        device_id_type=pl.DeviceIdType.MESH,
    )


def square():
    me = lax.axis_index("space")
    xn = me + 1 - 2 * (me % 2)
    yn = (me + 2) % 4
    return me, xn, yn, (xn + 2) % 4


def seg(gath, t, dev, first, count):
    return gath.at[pl.ds((dev * t + first) * 4, 4 * count)]


def send_tiles(gath, sems, t, first, count, i):
    me, xn, yn, _ = square()
    mine = seg(gath, t, me, first, count)
    remote(mine, mine, sems, i, {"space": xn}).start()
    remote(mine, mine, sems, t + i, {"space": yn}).start()


def relay_tiles(gath, sems, t, first, count, i, by_x):
    _, xn, yn, _ = square()
    source, target = (xn, yn) if by_x else (yn, xn)
    got = seg(gath, t, source, first, count)
    remote(got, got, sems, i if by_x else t + i, {"space": source}).wait_recv()
    remote(got, got, sems, 2 * t + i, {"space": target}).start()


def drain_tiles(gath, sems, t, first, count, i, by_x):
    me, xn, yn, dg = square()
    mine = seg(gath, t, me, first, count)
    remote(mine, mine, sems, i, {"space": xn}).wait_send()
    remote(mine, mine, sems, t + i, {"space": yn}).wait_send()
    source, other = (xn, yn) if by_x else (yn, xn)
    got = seg(gath, t, source, first, count)
    remote(got, got, sems, 2 * t + i, {"space": other}).wait_send()
    late = seg(gath, t, other, first, count)
    remote(late, late, sems, t + i if by_x else i, {"space": other}).wait_recv()
    far = seg(gath, t, dg, first, count)
    remote(far, far, sems, 2 * t + i, {"space": other}).wait_recv()


def put_strips(gath, t, i, field):
    me = lax.axis_index("space")
    base = (me * t + i) * 4
    s = field.shape[0]
    gath[base] = field[0].astype(BF16)
    gath[base + 1] = field[s - 1].astype(BF16)
    gath[base + 2] = field[:, 0, :].astype(BF16)
    gath[base + 3] = field[:, s - 1, :].astype(BF16)


def orient_tiles(gath, adj, out):
    t = out.shape[0]
    s = out.shape[2]
    r = lax.broadcasted_iota(jnp.int32, (s, s), 0)
    c = lax.broadcasted_iota(jnp.int32, (s, s), 1)
    turn = jnp.where(r + c == s - 1, 1.0, 0.0).astype(BF16)

    def body(a, carry):
        for e in range(4):
            line = gath[adj[a, e, 0] * 4 + adj[a, e, 1]]
            back = jnp.dot(turn, line, preferred_element_type=F32)
            out[a, e] = jnp.where(adj[a, e, 2] == 1, back, line.astype(F32)).astype(BF16)
        return carry

    lax.fori_loop(0, t, body, 0)


def stream_begin():
    _, xn, yn, _ = square()

    @pl.when(pl.program_id(0) == 0)
    def _():
        greet([{"space": xn}, {"space": yn}])


def stream_tile(gath, sems, t, adj, out):
    i = pl.program_id(0)
    h = t // 2
    send_tiles(gath, sems, t, i, 1, i)

    def relay(j):
        pl.when(j < h)(lambda: relay_tiles(gath, sems, t, j, 1, j, True))
        pl.when(j >= h)(lambda: relay_tiles(gath, sems, t, j, 1, j, False))

    pl.when(i > 0)(lambda: relay(i - 1))

    @pl.when(i == t - 1)
    def _():
        relay(i)
        for j in range(t):
            drain_tiles(gath, sems, t, j, 1, j, j < h)
        orient_tiles(gath, adj, out)


def greet(peers):
    barrier = pltpu.get_barrier_semaphore()
    for who in peers:
        pl.semaphore_signal(
            barrier, inc=1, device_id=who, device_id_type=pl.DeviceIdType.MESH
        )
    pl.semaphore_wait(barrier, len(peers))


def c_open(n_dp, w_in, x, adj, w_out, out, gath, sems, own, zs, ps):
    me, xn, yn, _ = square()
    line = n_dp // 2
    dp = lax.axis_index("dp")
    q, core = dp // 2, dp % 2
    depth = w_in.shape[3]
    layers = w_in.shape[0]
    right = {"dp": ((q + 1) % line) * 2 + core}
    left = {"dp": ((q + line - 1) % line) * 2 + core}
    partner = {"dp": q * 2 + 1 - core}
    greet([{"space": xn}, {"space": yn}, right, left, partner])
    t = x.shape[0]
    h = t // 2
    parts = ((0, h, True), (h, t - h, False))

    def build(a, carry):
        put_strips(gath, t, a, x[a].astype(F32))
        return carry

    def slot(l, o, c):
        return w_out.at[l, :, :, pl.ds(pl.multiple_of((o * 2 + c) * depth, depth), depth), :]

    keep = pltpu.make_async_copy(
        w_in, w_out.at[:, :, :, pl.ds(pl.multiple_of(dp * depth, depth), depth), :], own
    )
    keep.start()

    def move(l, o, who, sm, i, first):
        ref = w_in.at[l] if first else slot(l, o, core)
        return remote(ref, slot(l, o, core), sm, i, who)

    def zi(l, s, way):
        return (l * line + s) * 2 + way

    def forward(l, s, way, o, first):
        who = right if way == 0 else left
        ok = (q + 1 < line) if way == 0 else (q > 0)

        @pl.when(ok)
        def _():
            move(l, o, who, zs, zi(l, s, way), first).start()

    for l in range(layers):
        forward(l, 0, 0, q, True)
        forward(l, 0, 1, q, True)
        move(l, q, partner, ps, zi(l, 0, 0), True).start()
    lax.fori_loop(0, t, build, 0)
    for i, (first, count, _) in enumerate(parts):
        send_tiles(gath, sems, t, first, count, i)
    for l in range(layers):
        if l == 1:
            for i, (first, count, by_x) in enumerate(parts):
                relay_tiles(gath, sems, t, first, count, i, by_x)
        for s in range(1, line):
            for way in (0, 1):
                o = q - s if way == 0 else q + s
                ok = (o >= 0) if way == 0 else (o < line)

                @pl.when(ok)
                def _(l=l, s=s, way=way, o=o):
                    move(l, o, right, zs, zi(l, s - 1, way), False).wait_recv()
                    move(l, o, partner, ps, zi(l, s, way), False).start()
                    if s < line - 1:
                        forward(l, s, way, o, False)

    for l in range(layers):
        for s in range(line):
            for way in (0, 1):
                o = q - s if way == 0 else q + s
                ok = (o >= 0) if way == 0 else (o < line)
                if s == 0 and way == 1:
                    ok = None

                def part(l=l, s=s, way=way, o=o):
                    copy = move(l, o, partner, ps, zi(l, s, way), False)
                    copy.wait_send()
                    remote(
                        slot(l, o, 1 - core), slot(l, o, 1 - core), ps, zi(l, s, way), partner
                    ).wait_recv()

                if ok is not None:
                    pl.when(ok)(part)
                if s < line - 1:
                    sent = (
                        jnp.logical_and(o >= 0, q + 1 < line)
                        if way == 0
                        else jnp.logical_and(o < line, q > 0)
                    )

                    @pl.when(sent)
                    def _(l=l, s=s, way=way, o=o):
                        move(l, o, right, zs, zi(l, s, way), False).wait_send()

    for i, (first, count, by_x) in enumerate(parts):
        drain_tiles(gath, sems, t, first, count, i, by_x)
    keep.wait()
    orient_tiles(gath, adj, out)


def c_sum(n_dp, g, out, b1, x_out, x_in, keep2, y_out, y_in, keep3, z_out, z_in, a_out, a_in, sems):
    me, xn, yn, _ = square()
    line = n_dp // 2
    dp = lax.axis_index("dp")
    q, core = dp // 2, dp % 2
    rows = g.shape[2]
    rh = rows // 2
    ry = y_in.shape[1]
    partner = {"dp": q * 2 + 1 - core}
    zp = [{"dp": ((q + d) % line) * 2 + core} for d in range(1, line)]
    mx, my = me % 2, me // 2
    x_mine = pl.multiple_of(mx * rh, 16)
    x_give = pl.multiple_of((1 - mx) * rh, 16)
    y_mine = pl.multiple_of(my * (rh - ry), 16)
    y_give = pl.multiple_of((1 - my) * (rh - ry), 16)
    greet([{"space": xn}, {"space": yn}, partner] + zp)
    give = remote(g.at[:, 1 - core, pl.ds(x_give, rh)], b1.at[:, pl.ds(x_give, rh)], sems, 0, partner)
    give.start()
    have = remote(g.at[:, 1 - core, pl.ds(x_mine, rh)], b1.at[:, pl.ds(x_mine, rh)], sems, 1, partner)
    have.start()
    give.wait_recv()
    for l in range(line):
        x_out[l] = (
            g[l, core, pl.ds(x_give, rh)].astype(F32) + b1[l, pl.ds(x_give, rh)].astype(F32)
        ).astype(BF16)
    sx = remote(x_out, x_in, sems, 2, {"space": xn})
    sx.start()
    have.wait_recv()
    for l in range(line):
        keep2[l] = g[l, core, pl.ds(x_mine, rh)].astype(F32) + b1[l, pl.ds(x_mine, rh)].astype(F32)
    sx.wait_recv()
    for l in range(line):
        y_out[l] = (
            keep2[l, pl.ds(y_give, ry)] + x_in[l, pl.ds(y_give, ry)].astype(F32)
        ).astype(BF16)
    sy = remote(y_out, y_in, sems, 3, {"space": yn})
    sy.start()
    for l in range(line):
        keep3[l] = keep2[l, pl.ds(y_mine, ry)] + x_in[l, pl.ds(y_mine, ry)].astype(F32)
    sy.wait_recv()
    for l in range(line):
        keep3[l] = keep3[l] + y_in[l].astype(F32)
    z_out[...] = keep3[...].astype(BF16)
    moves = []
    for d in range(1, line):
        copy = remote(z_out.at[(q + d) % line], z_in.at[d - 1], sems, 3 + d, zp[d - 1])
        copy.start()
        moves.append(copy)
    total = keep3[q]
    for d, copy in enumerate(moves):
        copy.wait_recv()
        total = total + z_in[d].astype(F32)
    a_out[...] = total.astype(BF16)
    back = pl.multiple_of(x_mine + y_mine, 16)
    fy = remote(a_out, a_in.at[0, pl.ds(0, ry)], sems, 3 + line, {"space": yn})
    fy.start()
    fx = remote(a_out, a_in.at[1, pl.ds(0, ry)], sems, 4 + line, {"space": xn})
    fx.start()
    fy.wait_recv()
    fz = remote(a_in.at[0, pl.ds(0, ry)], a_in.at[2, pl.ds(0, ry)], sems, 5 + line, {"space": xn})
    fz.start()
    out[pl.ds(back, ry)] = a_out[...].astype(F32)
    out[pl.ds(pl.multiple_of(x_mine + y_give, 16), ry)] = a_in[0].astype(F32)
    fx.wait_recv()
    out[pl.ds(pl.multiple_of(x_give + y_mine, 16), ry)] = a_in[1].astype(F32)
    fz.wait_recv()
    out[pl.ds(pl.multiple_of(x_give + y_give, 16), ry)] = a_in[2].astype(F32)
    for copy in [give, have, sx, sy, fy, fx, fz] + moves:
        copy.wait_send()


VM = pl.BlockSpec(memory_space=pltpu.VMEM)


def params(cid):
    return pltpu.CompilerParams(
        collective_id=cid, has_side_effects=True, vmem_limit_bytes=60 << 20
    )


def open_gather(n_dp, kernels, x, adjacency):
    dma = pltpu.SemaphoreType.DMA
    shape = kernels.shape
    whole = shape[:3] + (shape[3] * n_dp, shape[4])
    return pl.pallas_call(
        functools.partial(c_open, n_dp),
        out_shape=(
            jax.ShapeDtypeStruct(whole, kernels.dtype),
            jax.ShapeDtypeStruct((x.shape[0], 4) + x.shape[2:], x.dtype),
        ),
        in_specs=[VM, VM, pl.BlockSpec(memory_space=pltpu.SMEM)],
        out_specs=(VM, VM),
        scratch_shapes=[
            pltpu.VMEM((16 * x.shape[0],) + x.shape[2:], x.dtype),
            dma((2, 3 * x.shape[0])),
            dma,
            dma((2, 2 * n_dp)),
            dma((2, 2 * n_dp)),
        ],
        compiler_params=params(0),
    )(kernels, x, adjacency)


def sum_grads(n_dp, g, cid):
    line = n_dp // 2
    rows, c = g.shape[1:]
    g = g.reshape(line, 2, rows, c)
    rh = rows // 2
    ry = -(-(rh // 2) // 16) * 16
    vm = pltpu.VMEM
    return pl.pallas_call(
        functools.partial(c_sum, n_dp),
        out_shape=jax.ShapeDtypeStruct((rows, c), F32),
        in_specs=[VM],
        out_specs=VM,
        scratch_shapes=[
            vm((line, rows, c), BF16),
            vm((line, rh, c), BF16),
            vm((line, rh, c), BF16),
            vm((line, rh, c), F32),
            vm((line, ry, c), BF16),
            vm((line, ry, c), BF16),
            vm((line, ry, c), F32),
            vm((line, ry, c), BF16),
            vm((line - 1, ry, c), BF16),
            vm((ry, c), BF16),
            vm((3, ry, c), BF16),
            pltpu.SemaphoreType.DMA((2, 6 + line)),
        ],
        compiler_params=params(cid),
    )(g)


def per_device(n_dp, n_sp, inputs, kernels, cotangent, adjacency):
    _, t, s, _, c = inputs.shape
    x0 = inputs[0]
    cot = cotangent[0]
    if n_sp == 4:
        weights, rims0 = open_gather(n_dp, kernels, x0, adjacency)
    else:
        weights = lax.all_gather(kernels, "dp", axis=3, tiled=True)
        rims0 = exchange(edge_strips(x0), adjacency)
    w1 = weights[0].reshape(3, 3 * c, c)
    w2 = weights[1].reshape(3, 3 * c, c)
    wt = jnp.transpose(weights[1][::-1, ::-1], (0, 1, 3, 2)).reshape(3, 3 * c, c)

    tile = pl.BlockSpec((1, s, s, c), lambda i: (i, 0, 0, 0))
    rim = pl.BlockSpec((1, 4, s, c), lambda i: (i, 0, 0, 0))
    wsp = pl.BlockSpec((3, 3 * c, c), lambda i: (0, 0, 0), pipeline_mode=pl.Buffered(1))
    field = lambda dt: jax.ShapeDtypeStruct((t, s, s, c), dt)
    dws = jax.ShapeDtypeStruct((n_dp, 9 * c // n_dp, c), BF16)
    dwsp = pl.BlockSpec(dws.shape, lambda i: (0, 0, 0))
    x3s = pltpu.VMEM((s + 2, s, 3 * c), BF16)
    accs = pltpu.VMEM((3, c, 3 * c), F32)
    flops = 2 * t * s * s * c * c * 9
    plain = pltpu.CompilerParams(vmem_limit_bytes=60 << 20)
    call = lambda body, nf, ins, outs, shapes, scratch, extra=plain: pl.pallas_call(
        body,
        grid=(t,),
        in_specs=ins,
        out_specs=outs,
        out_shape=shapes,
        scratch_shapes=scratch,
        compiler_params=extra,
        cost_estimate=pl.CostEstimate(
            flops=nf * flops, bytes_accessed=12 << 20, transcendentals=0
        ),
    )
    rims = jax.ShapeDtypeStruct((t, 4, s, c), BF16)
    if n_sp == 4:
        smem = pl.BlockSpec(memory_space=pltpu.SMEM)
        whole = pl.BlockSpec((t, 4, s, c), lambda i: (0, 0, 0, 0))
        passing = [
            pltpu.VMEM((16 * t, s, c), BF16),
            pltpu.SemaphoreType.DMA((2, 3 * t)),
        ]
        state1, slope1, rims1 = call(
            k_first_send,
            1,
            [tile, rim, wsp, smem],
            [tile, tile, whole],
            [field(BF16), field(F32), rims],
            [x3s] + passing,
            params(1),
        )(x0, rims0, w1, adjacency)
        state2, g2, back = call(
            k_last_send,
            1,
            [tile, rim, wsp, wsp, tile, smem],
            [tile, tile, whole],
            [field(BF16), field(BF16), rims],
            [x3s, x3s, pltpu.VMEM((1, 4, s, c), BF16)] + passing,
            params(2),
        )(state1, rims1, w2, wt, cot, adjacency)
    else:
        state1, slope1 = call(
            k_first_only, 1, [tile, rim, wsp], [tile, tile], [field(BF16), field(F32)], [x3s]
        )(x0, rims0, w1)
        rims1 = exchange(edge_strips(state1), adjacency)
        state2, g2, rg = call(
            k_last,
            1,
            [tile, rim, wsp, wsp, tile],
            [tile, tile, rim],
            [field(BF16), field(BF16), rims],
            [x3s, x3s],
        )(state1, rims1, w2, wt, cot)
        back = exchange(rg, adjacency)
    up, dw2 = call(
        k_back, 2, [tile, rim, tile, wsp, tile], [tile, dwsp], [field(F32), dws], [x3s, x3s, accs]
    )(state1, rims1, g2, wt, cot)
    dw1 = call(k_tail, 1, [tile, rim, tile, rim, tile], dwsp, dws, [x3s, accs])(
        x0, rims0, up, back, slope1
    )
    return state2[None], reduce_grads(dw1, dw2, n_dp, n_sp)


def solution(mesh):
    in_specs = (
        P("dp", "space", None, None, None),
        P(None, None, None, "dp", None),
        P("dp", "space", None, None, None),
        P("space", None, None),
    )
    out_specs = (P("dp", "space", None, None, None), P(None, None, None, "dp", None))
    body = functools.partial(per_device, mesh.shape["dp"], mesh.shape["space"])
    return jax.shard_map(
        body, mesh=mesh, in_specs=in_specs, out_specs=out_specs, check_vma=False
    )
```

```python
import functools

import jax
import jax.numpy as jnp
from jax import lax
from jax.experimental import pallas as pl
from jax.experimental.pallas import tpu as pltpu
from jax.sharding import PartitionSpec as P

LAYERS = 2
F32 = jnp.float32
BF16 = jnp.bfloat16


def edge_strips(field):
    return jnp.stack(
        [field[:, 0], field[:, -1], field[:, :, 0], field[:, :, -1]], axis=1
    )


def orient(strips, adjacency):
    selected = strips[adjacency[:, :, 0], adjacency[:, :, 1]]
    flipped = (adjacency[:, :, 2] == 1)[:, :, None, None]
    return jnp.where(flipped, selected[:, :, ::-1], selected)


def exchange(strips, adjacency):
    return orient(lax.all_gather(strips, "space", axis=0, tiled=True), adjacency)


def fill(x3, field, rims):
    s, _, c = field.shape
    col = lax.broadcasted_iota(jnp.int32, (s, s, c), 1)
    wide = field.astype(F32)
    if rims is None:
        left = right = jnp.zeros((1, 1, 1), F32)
    else:
        left = rims[2].astype(F32)[:, None, :]
        right = rims[3].astype(F32)[:, None, :]
    x3[1 : s + 1, :, c : 2 * c] = field
    x3[1 : s + 1, :, 0:c] = jnp.where(col == 0, left, pltpu.roll(wide, 1, 1)).astype(BF16)
    x3[1 : s + 1, :, 2 * c :] = jnp.where(
        col == s - 1, right, pltpu.roll(wide, s - 1, 1)
    ).astype(BF16)
    rc = lax.broadcasted_iota(jnp.int32, (s, c), 0)
    for row, edge in ((0, 0), (s + 1, 1)):
        if rims is None:
            x3[row] = jnp.zeros((s, 3 * c), BF16)
        else:
            line = rims[edge].astype(F32)
            x3[row, :, c : 2 * c] = rims[edge]
            x3[row, :, 0:c] = jnp.where(rc == 0, 0.0, pltpu.roll(line, 1, 0)).astype(BF16)
            x3[row, :, 2 * c :] = jnp.where(
                rc == s - 1, 0.0, pltpu.roll(line, s - 1, 0)
            ).astype(BF16)


def conv(x3, w):
    s = x3.shape[1]
    k = x3.shape[2]
    total = None
    for p in range(3):
        part = jnp.dot(
            x3[p : p + s].reshape(s * s, k), w[p], preferred_element_type=F32
        )
        total = part if total is None else total + part
    return total.reshape(s, s, -1)


def wgrad_add(acc, x3, grad):
    s = x3.shape[1]
    k = x3.shape[2]
    flipped = grad.reshape(s * s, -1).T
    for p in range(3):
        acc[p] += jnp.dot(
            flipped, x3[p : p + s].reshape(s * s, k), preferred_element_type=F32
        )


def k_first_send(x, rims, w, adj, state, slope, rims_out, x3, gath, sems):
    stream_begin()
    t = rims_out.shape[0]
    out = k_first(x, rims, w, state, slope, x3)
    put_strips(gath, t, pl.program_id(0), out)
    stream_tile(gath, sems, t, adj, rims_out)


def k_first_only(*refs):
    k_first(*refs)


def turn_weights(w, wt):
    c = w.shape[2]
    for p in range(3):
        for q in range(3):
            tap = w[2 - p, (2 - q) * c : (3 - q) * c]
            wt[p, q * c : (q + 1) * c] = tap.astype(F32).T.astype(BF16)


def k_last_send(
    x, rims, w, cot, adj, state, grad, back, dw, x3, g3, rim_grad, wt, held, acc, gath, sems
):
    t = back.shape[0]
    i = pl.program_id(0)
    stream_begin()

    @pl.when(i == 0)
    def _():
        turn_weights(w, wt)
        acc[...] = jnp.zeros_like(acc)

    fill(x3, x[0], rims[0])

    @pl.when(i < t)
    def _():
        k_last(x, rims, w, wt, cot, state, grad, rim_grad, x3, g3, False)
        held[i] = grad[0]
        me = lax.axis_index("space")
        base = (me * t + i) * 4
        for e in range(4):
            gath[base + e] = rim_grad[0, e]

    stream_tile(gath, sems, t, adj, back, True)

    @pl.when(i >= t)
    def _():
        wgrad_add(acc, x3, held[i - t])

    finish_wgrad(acc, dw)


def k_tail_send(
    n_dp, x, rims, g, w, cot, back, slope, dw2, dw, out, x3, g3, wt, acc, *sums
):
    i = pl.program_id(0)
    last = pl.num_programs(0) - 1
    peers, stages = sum_stages(n_dp, dw2, out, *sums)

    @pl.when(i == 0)
    def _():
        greet(peers)
        stages[0]()
        turn_weights(w, wt)
        acc[...] = jnp.zeros_like(acc)

    for k, stage in enumerate(stages[1:-1]):
        pl.when(i == jnp.minimum(k + 1, last))(stage)
    fill(g3, g[0], None)
    tail_tile(x, rims, cot[0].astype(F32) + conv(g3, wt), back, slope, x3, acc)
    pl.when(i == last)(stages[-1])
    finish_wgrad(acc, dw)


def k_first(x, rims, w, state, slope, x3):
    fill(x3, x[0], rims[0])
    v = conv(x3, w)
    sg = jax.nn.sigmoid(v)
    out = x[0].astype(F32) + v * sg
    state[0] = out.astype(BF16)
    slope[0] = (sg * (1.0 + v * (1.0 - sg))).astype(slope.dtype)
    return out


def k_last(x, rims, w, wt, cot, state, grad, rim_grad, x3, g3, build=True):
    s = x.shape[1]
    c = x.shape[3]
    if build:
        fill(x3, x[0], rims[0])
    v = conv(x3, w)
    sg = jax.nn.sigmoid(v)
    state[0] = (x[0].astype(F32) + v * sg).astype(BF16)
    g32 = cot[0].astype(F32) * (sg * (1.0 + v * (1.0 - sg)))
    g = g32.astype(BF16)
    grad[0] = g
    fill(g3, g, None)
    rim_grad[0, 0] = jnp.dot(g3[1], wt[2], preferred_element_type=F32).astype(BF16)
    rim_grad[0, 1] = jnp.dot(g3[s], wt[0], preferred_element_type=F32).astype(BF16)
    for edge, col, q in ((2, 0, 2), (3, s - 1, 0)):
        line = jnp.concatenate(
            [g3[p : p + s, :, c : 2 * c].astype(F32)[:, col, :] for p in range(3)], axis=1
        ).astype(BF16)
        weight = jnp.concatenate([wt[p, q * c : (q + 1) * c] for p in range(3)], axis=0)
        rim_grad[0, edge] = jnp.dot(line, weight, preferred_element_type=F32).astype(BF16)


def finish_wgrad(acc, out):
    @pl.when(pl.program_id(0) == pl.num_programs(0) - 1)
    def _():
        n, _, c = out.shape
        depth = c // n
        for p in range(3):
            for q in range(3):
                tap = acc[p, :, q * c : (q + 1) * c].T.astype(out.dtype)
                first = (3 * p + q) * depth
                out[:, first : first + depth, :] = tap.reshape(n, depth, c)


def k_back(x, rims, g, wt, cot, up, dw, x3, g3, acc):
    @pl.when(pl.program_id(0) == 0)
    def _():
        acc[...] = jnp.zeros_like(acc)

    fill(x3, x[0], rims[0])
    wgrad_add(acc, x3, g[0])
    fill(g3, g[0], None)
    up[0] = cot[0].astype(F32) + conv(g3, wt)
    finish_wgrad(acc, dw)


def tail_tile(x, rims, u, back, slope, x3, acc):
    s = x.shape[1]
    fill(x3, x[0], rims[0])
    row = lax.broadcasted_iota(jnp.int32, u.shape, 0)
    col = lax.broadcasted_iota(jnp.int32, u.shape, 1)
    r = back[0].astype(F32)
    u = u + jnp.where(row == 0, r[0][None], 0.0) + jnp.where(row == s - 1, r[1][None], 0.0)
    u = u + jnp.where(col == 0, r[2][:, None, :], 0.0)
    u = u + jnp.where(col == s - 1, r[3][:, None, :], 0.0)
    g = (u * slope[0].astype(F32)).astype(BF16)
    wgrad_add(acc, x3, g)


def k_tail(x, rims, up, back, slope, dw, x3, acc):
    @pl.when(pl.program_id(0) == 0)
    def _():
        acc[...] = jnp.zeros_like(acc)

    tail_tile(x, rims, up[0], back, slope, x3, acc)
    finish_wgrad(acc, dw)


def reduce_grads(dw1, dw2, n_dp):
    both = jnp.concatenate([dw1, dw2], axis=1)
    n, rows, c = both.shape
    part = lax.psum_scatter(both.astype(F32), "dp", scatter_dimension=0, tiled=True)
    return lax.psum(part, "space").reshape(LAYERS, 3, 3, c // n, c)


def remote(src, dst, sems, i, who):
    return pltpu.make_async_remote_copy(
        src_ref=src,
        dst_ref=dst,
        send_sem=sems.at[0, i],
        recv_sem=sems.at[1, i],
        device_id=who,
        device_id_type=pl.DeviceIdType.MESH,
    )


def square():
    me = lax.axis_index("space")
    xn = me + 1 - 2 * (me % 2)
    yn = (me + 2) % 4
    return me, xn, yn, (xn + 2) % 4


def seg(gath, t, dev, first, count):
    return gath.at[pl.ds((dev * t + first) * 4, 4 * count)]


def send_tiles(gath, sems, t, first, count, i):
    me, xn, yn, _ = square()
    mine = seg(gath, t, me, first, count)
    remote(mine, mine, sems, i, {"space": xn}).start()
    remote(mine, mine, sems, t + i, {"space": yn}).start()


def relay_tiles(gath, sems, t, first, count, i, by_x):
    _, xn, yn, _ = square()
    source, target = (xn, yn) if by_x else (yn, xn)
    got = seg(gath, t, source, first, count)
    remote(got, got, sems, i if by_x else t + i, {"space": source}).wait_recv()
    remote(got, got, sems, 2 * t + i, {"space": target}).start()


def drain_tiles(gath, sems, t, first, count, i, by_x):
    me, xn, yn, dg = square()
    mine = seg(gath, t, me, first, count)
    remote(mine, mine, sems, i, {"space": xn}).wait_send()
    remote(mine, mine, sems, t + i, {"space": yn}).wait_send()
    source, other = (xn, yn) if by_x else (yn, xn)
    got = seg(gath, t, source, first, count)
    remote(got, got, sems, 2 * t + i, {"space": other}).wait_send()
    late = seg(gath, t, other, first, count)
    remote(late, late, sems, t + i if by_x else i, {"space": other}).wait_recv()
    far = seg(gath, t, dg, first, count)
    remote(far, far, sems, 2 * t + i, {"space": other}).wait_recv()


def put_strips(gath, t, i, field):
    me = lax.axis_index("space")
    base = (me * t + i) * 4
    s = field.shape[0]
    gath[base] = field[0].astype(BF16)
    gath[base + 1] = field[s - 1].astype(BF16)
    gath[base + 2] = field[:, 0, :].astype(BF16)
    gath[base + 3] = field[:, s - 1, :].astype(BF16)


def orient_tiles(gath, adj, out):
    t = out.shape[0]
    s = out.shape[2]
    r = lax.broadcasted_iota(jnp.int32, (s, s), 0)
    c = lax.broadcasted_iota(jnp.int32, (s, s), 1)
    turn = jnp.where(r + c == s - 1, 1.0, 0.0).astype(BF16)

    def body(a, carry):
        for e in range(4):
            line = gath[adj[a, e, 0] * 4 + adj[a, e, 1]]
            back = jnp.dot(turn, line, preferred_element_type=F32)
            out[a, e] = jnp.where(adj[a, e, 2] == 1, back, line.astype(F32)).astype(BF16)
        return carry

    lax.fori_loop(0, t, body, 0)


def stream_begin():
    _, xn, yn, _ = square()

    @pl.when(pl.program_id(0) == 0)
    def _():
        greet([{"space": xn}, {"space": yn}])


def stream_tile(gath, sems, t, adj, out, phases=False):
    i = pl.program_id(0)
    h = t // 2

    def relay(j):
        pl.when(j < h)(lambda: relay_tiles(gath, sems, t, j, 1, j, True))
        pl.when(j >= h)(lambda: relay_tiles(gath, sems, t, j, 1, j, False))

    @pl.when(i < t)
    def _():
        send_tiles(gath, sems, t, i, 1, i)

    if phases:
        pl.when(jnp.logical_and(i > 1, i < t + 2))(lambda: relay(i - 2))
    else:
        pl.when(i > 0)(lambda: relay(i - 1))

    @pl.when(i == pl.num_programs(0) - 1)
    def _():
        if not phases:
            relay(i)
        for j in range(t):
            drain_tiles(gath, sems, t, j, 1, j, j < h)
        orient_tiles(gath, adj, out)


def greet(peers):
    barrier = pltpu.get_barrier_semaphore()
    for who in peers:
        pl.semaphore_signal(
            barrier, inc=1, device_id=who, device_id_type=pl.DeviceIdType.MESH
        )
    pl.semaphore_wait(barrier, len(peers))


def c_open(n_dp, w_in, x, adj, w_out, out, gath, sems, own, zs, ps):
    me, xn, yn, _ = square()
    line = n_dp // 2
    dp = lax.axis_index("dp")
    q, core = dp // 2, dp % 2
    depth = w_in.shape[3]
    layers = w_in.shape[0]
    right = {"dp": ((q + 1) % line) * 2 + core}
    left = {"dp": ((q + line - 1) % line) * 2 + core}
    partner = {"dp": q * 2 + 1 - core}
    greet([{"space": xn}, {"space": yn}, right, left, partner])
    t = x.shape[0]
    h = t // 2
    parts = ((0, h, True), (h, t - h, False))

    def build(a, carry):
        put_strips(gath, t, a, x[a].astype(F32))
        return carry

    def slot(l, o, c):
        return w_out.at[l, :, :, pl.ds(pl.multiple_of((o * 2 + c) * depth, depth), depth), :]

    keep = pltpu.make_async_copy(
        w_in, w_out.at[:, :, :, pl.ds(pl.multiple_of(dp * depth, depth), depth), :], own
    )
    keep.start()

    def move(l, o, who, sm, i, first):
        ref = w_in.at[l] if first else slot(l, o, core)
        return remote(ref, slot(l, o, core), sm, i, who)

    def zi(l, s, way):
        return (l * line + s) * 2 + way

    def forward(l, s, way, o, first):
        who = right if way == 0 else left
        ok = (q + 1 < line) if way == 0 else (q > 0)

        @pl.when(ok)
        def _():
            move(l, o, who, zs, zi(l, s, way), first).start()

    for l in range(layers):
        forward(l, 0, 0, q, True)
        forward(l, 0, 1, q, True)
        move(l, q, partner, ps, zi(l, 0, 0), True).start()
    lax.fori_loop(0, t, build, 0)
    for i, (first, count, _) in enumerate(parts):
        send_tiles(gath, sems, t, first, count, i)
    for l in range(layers):
        if l == 1:
            for i, (first, count, by_x) in enumerate(parts):
                relay_tiles(gath, sems, t, first, count, i, by_x)
        for s in range(1, line):
            for way in (0, 1):
                o = q - s if way == 0 else q + s
                ok = (o >= 0) if way == 0 else (o < line)

                @pl.when(ok)
                def _(l=l, s=s, way=way, o=o):
                    move(l, o, right, zs, zi(l, s - 1, way), False).wait_recv()
                    move(l, o, partner, ps, zi(l, s, way), False).start()
                    if s < line - 1:
                        forward(l, s, way, o, False)

    for l in range(layers):
        for s in range(line):
            for way in (0, 1):
                o = q - s if way == 0 else q + s
                ok = (o >= 0) if way == 0 else (o < line)
                if s == 0 and way == 1:
                    ok = None

                def part(l=l, s=s, way=way, o=o):
                    copy = move(l, o, partner, ps, zi(l, s, way), False)
                    copy.wait_send()
                    remote(
                        slot(l, o, 1 - core), slot(l, o, 1 - core), ps, zi(l, s, way), partner
                    ).wait_recv()

                if ok is not None:
                    pl.when(ok)(part)
                if s < line - 1:
                    sent = (
                        jnp.logical_and(o >= 0, q + 1 < line)
                        if way == 0
                        else jnp.logical_and(o < line, q > 0)
                    )

                    @pl.when(sent)
                    def _(l=l, s=s, way=way, o=o):
                        move(l, o, right, zs, zi(l, s, way), False).wait_send()

    for i, (first, count, by_x) in enumerate(parts):
        drain_tiles(gath, sems, t, first, count, i, by_x)
    keep.wait()
    orient_tiles(gath, adj, out)


def sum_stages(
    n_dp, g, out, b1, x_out, x_in, keep2, y_out, y_in, keep3, z_out, z_in, a_out, a_in, sems
):
    me, xn, yn, _ = square()
    line = n_dp // 2
    dp = lax.axis_index("dp")
    q, core = dp // 2, dp % 2
    rows = g.shape[2]
    rh = rows // 2
    ry = y_in.shape[1]
    partner = {"dp": q * 2 + 1 - core}
    zp = [{"dp": ((q + d) % line) * 2 + core} for d in range(1, line)]
    mx, my = me % 2, me // 2
    x_mine = pl.multiple_of(mx * rh, 16)
    x_give = pl.multiple_of((1 - mx) * rh, 16)
    y_mine = pl.multiple_of(my * (rh - ry), 16)
    y_give = pl.multiple_of((1 - my) * (rh - ry), 16)
    peers = [{"space": xn}, {"space": yn}, partner] + zp

    def half(first, i):
        return remote(
            g.at[:, 1 - core, pl.ds(first, rh)], b1.at[:, pl.ds(first, rh)], sems, i, partner
        )

    give = lambda: half(x_give, 0)
    have = lambda: half(x_mine, 1)
    sx = lambda: remote(x_out, x_in, sems, 2, {"space": xn})
    sy = lambda: remote(y_out, y_in, sems, 3, {"space": yn})
    sz = lambda d: remote(z_out.at[(q + d) % line], z_in.at[d - 1], sems, 3 + d, zp[d - 1])
    fy = lambda: remote(a_out, a_in.at[0], sems, 3 + line, {"space": yn})
    fx = lambda: remote(a_out, a_in.at[1], sems, 4 + line, {"space": xn})
    fz = lambda: remote(a_in.at[0], a_in.at[2], sems, 5 + line, {"space": xn})

    def s0():
        give().start()
        have().start()

    def s1():
        give().wait_recv()
        for l in range(line):
            x_out[l] = (
                g[l, core, pl.ds(x_give, rh)].astype(F32) + b1[l, pl.ds(x_give, rh)].astype(F32)
            ).astype(BF16)
        sx().start()
        have().wait_recv()
        for l in range(line):
            keep2[l] = g[l, core, pl.ds(x_mine, rh)].astype(F32) + b1[
                l, pl.ds(x_mine, rh)
            ].astype(F32)

    def s2():
        sx().wait_recv()
        for l in range(line):
            y_out[l] = (
                keep2[l, pl.ds(y_give, ry)] + x_in[l, pl.ds(y_give, ry)].astype(F32)
            ).astype(BF16)
        sy().start()
        for l in range(line):
            keep3[l] = keep2[l, pl.ds(y_mine, ry)] + x_in[l, pl.ds(y_mine, ry)].astype(F32)

    def s3():
        sy().wait_recv()
        for l in range(line):
            keep3[l] = keep3[l] + y_in[l].astype(F32)
        z_out[...] = keep3[...].astype(BF16)
        for d in range(1, line):
            sz(d).start()

    def s4():
        total = keep3[q]
        for d in range(1, line):
            sz(d).wait_recv()
            total = total + z_in[d - 1].astype(F32)
        a_out[...] = total.astype(BF16)
        fy().start()
        fx().start()

    def s5():
        fy().wait_recv()
        fz().start()
        out[pl.ds(pl.multiple_of(x_mine + y_mine, 16), ry)] = a_out[...].astype(F32)
        out[pl.ds(pl.multiple_of(x_mine + y_give, 16), ry)] = a_in[0].astype(F32)
        fx().wait_recv()
        out[pl.ds(pl.multiple_of(x_give + y_mine, 16), ry)] = a_in[1].astype(F32)
        fz().wait_recv()
        out[pl.ds(pl.multiple_of(x_give + y_give, 16), ry)] = a_in[2].astype(F32)
        for copy in [give, have, sx, sy, fy, fx, fz]:
            copy().wait_send()
        for d in range(1, line):
            sz(d).wait_send()

    return peers, [s0, s1, s2, s3, s4, s5]


def c_sum(n_dp, *refs):
    peers, stages = sum_stages(n_dp, *refs)
    greet(peers)
    for stage in stages:
        stage()


def sum_scratch(n_dp, rows, c):
    line = n_dp // 2
    rh = rows // 2
    ry = -(-(rh // 2) // 16) * 16
    vm = pltpu.VMEM
    return [
        vm((line, rows, c), BF16),
        vm((line, rh, c), BF16),
        vm((line, rh, c), BF16),
        vm((line, rh, c), F32),
        vm((line, ry, c), BF16),
        vm((line, ry, c), BF16),
        vm((line, ry, c), F32),
        vm((line, ry, c), BF16),
        vm((line - 1, ry, c), BF16),
        vm((ry, c), BF16),
        vm((3, ry, c), BF16),
        pltpu.SemaphoreType.DMA((2, 6 + line)),
    ]


VM = pl.BlockSpec(memory_space=pltpu.VMEM)


def params(cid):
    return pltpu.CompilerParams(
        collective_id=cid, has_side_effects=True, vmem_limit_bytes=60 << 20
    )


def open_gather(n_dp, kernels, x, adjacency):
    dma = pltpu.SemaphoreType.DMA
    shape = kernels.shape
    whole = shape[:3] + (shape[3] * n_dp, shape[4])
    return pl.pallas_call(
        functools.partial(c_open, n_dp),
        out_shape=(
            jax.ShapeDtypeStruct(whole, kernels.dtype),
            jax.ShapeDtypeStruct((x.shape[0], 4) + x.shape[2:], x.dtype),
        ),
        in_specs=[VM, VM, pl.BlockSpec(memory_space=pltpu.SMEM)],
        out_specs=(VM, VM),
        scratch_shapes=[
            pltpu.VMEM((16 * x.shape[0],) + x.shape[2:], x.dtype),
            dma((2, 3 * x.shape[0])),
            dma,
            dma((2, 2 * n_dp)),
            dma((2, 2 * n_dp)),
        ],
        compiler_params=params(0),
    )(kernels, x, adjacency)


def sum_grads(n_dp, g, cid):
    line = n_dp // 2
    rows, c = g.shape[1:]
    return pl.pallas_call(
        functools.partial(c_sum, n_dp),
        out_shape=jax.ShapeDtypeStruct((rows, c), F32),
        in_specs=[VM],
        out_specs=VM,
        scratch_shapes=sum_scratch(n_dp, rows, c),
        compiler_params=params(cid),
    )(g.reshape(line, 2, rows, c))


def per_device(n_dp, n_sp, inputs, kernels, cotangent, adjacency):
    _, t, s, _, c = inputs.shape
    x0 = inputs[0]
    cot = cotangent[0]
    if n_sp == 4:
        weights, rims0 = open_gather(n_dp, kernels, x0, adjacency)
    else:
        weights = lax.all_gather(kernels, "dp", axis=3, tiled=True)
        rims0 = exchange(edge_strips(x0), adjacency)
    w1 = weights[0].reshape(3, 3 * c, c)
    w2 = weights[1].reshape(3, 3 * c, c)
    wt = jnp.transpose(weights[1][::-1, ::-1], (0, 1, 3, 2)).reshape(3, 3 * c, c)

    tile = pl.BlockSpec((1, s, s, c), lambda i: (i, 0, 0, 0))
    rim = pl.BlockSpec((1, 4, s, c), lambda i: (i, 0, 0, 0))
    wsp = pl.BlockSpec((3, 3 * c, c), lambda i: (0, 0, 0), pipeline_mode=pl.Buffered(1))
    field = lambda dt: jax.ShapeDtypeStruct((t, s, s, c), dt)
    dws = jax.ShapeDtypeStruct((n_dp, 9 * c // n_dp, c), BF16)
    dwsp = pl.BlockSpec(dws.shape, lambda i: (0, 0, 0))
    x3s = pltpu.VMEM((s + 2, s, 3 * c), BF16)
    accs = pltpu.VMEM((3, c, 3 * c), F32)
    flops = 2 * t * s * s * c * c * 9
    plain = pltpu.CompilerParams(vmem_limit_bytes=60 << 20)
    call = lambda body, nf, ins, outs, shapes, scratch, extra=plain, steps=t: pl.pallas_call(
        body,
        grid=(steps,),
        in_specs=ins,
        out_specs=outs,
        out_shape=shapes,
        scratch_shapes=scratch,
        compiler_params=extra,
        cost_estimate=pl.CostEstimate(
            flops=nf * flops, bytes_accessed=12 << 20, transcendentals=0
        ),
    )
    rims = jax.ShapeDtypeStruct((t, 4, s, c), BF16)
    if n_sp == 4:
        smem = pl.BlockSpec(memory_space=pltpu.SMEM)
        whole = pl.BlockSpec((t, 4, s, c), lambda i: (0, 0, 0, 0))
        passing = [
            pltpu.VMEM((16 * t, s, c), BF16),
            pltpu.SemaphoreType.DMA((2, 3 * t)),
        ]
        state1, slope1, rims1 = call(
            k_first_send,
            1,
            [tile, rim, wsp, smem],
            [tile, tile, whole],
            [field(BF16), field(F32), rims],
            [x3s] + passing,
            params(1),
        )(x0, rims0, w1, adjacency)
        twice = pl.BlockSpec((1, s, s, c), lambda i: (i % t, 0, 0, 0))
        rim2 = pl.BlockSpec((1, 4, s, c), lambda i: (i % t, 0, 0, 0))
        once = pl.BlockSpec((1, s, s, c), lambda i: (jnp.minimum(i, t - 1), 0, 0, 0))
        wts = pltpu.VMEM((3, 3 * c, c), BF16)
        state2, g2, back, dw2 = call(
            k_last_send,
            2,
            [twice, rim2, wsp, once, smem],
            [once, once, whole, dwsp],
            [field(BF16), field(BF16), rims, dws],
            [x3s, x3s, pltpu.VMEM((1, 4, s, c), BF16), wts, pltpu.VMEM((t, s, s, c), BF16), accs]
            + passing,
            params(2),
            2 * t,
        )(state1, rims1, w2, cot, adjacency)
        rows = dws.shape[1]
        line = n_dp // 2
        wide = pl.BlockSpec((line, 2, rows, c), lambda i: (0, 0, 0, 0))
        flat = pl.BlockSpec((rows, c), lambda i: (0, 0))
        total = jax.ShapeDtypeStruct((rows, c), F32)
        dw1, sum2 = call(
            functools.partial(k_tail_send, n_dp),
            2,
            [tile, rim, tile, wsp, tile, rim, tile, wide],
            [dwsp, flat],
            [dws, total],
            [x3s, x3s, wts, accs] + sum_scratch(n_dp, rows, c),
            params(4),
        )(x0, rims0, g2, w2, cot, back, slope1, dw2.reshape(line, 2, rows, c))
        sum1 = sum_grads(n_dp, dw1, 3)
        grads = jnp.stack([sum1, sum2]).reshape(LAYERS, 3, 3, c // n_dp, c)
    else:
        state1, slope1 = call(
            k_first_only, 1, [tile, rim, wsp], [tile, tile], [field(BF16), field(F32)], [x3s]
        )(x0, rims0, w1)
        rims1 = exchange(edge_strips(state1), adjacency)
        state2, g2, rg = call(
            k_last,
            1,
            [tile, rim, wsp, wsp, tile],
            [tile, tile, rim],
            [field(BF16), field(BF16), rims],
            [x3s, x3s],
        )(state1, rims1, w2, wt, cot)
        back = exchange(rg, adjacency)
        up, dw2 = call(
            k_back,
            2,
            [tile, rim, tile, wsp, tile],
            [tile, dwsp],
            [field(F32), dws],
            [x3s, x3s, accs],
        )(state1, rims1, g2, wt, cot)
        dw1 = call(k_tail, 1, [tile, rim, tile, rim, tile], dwsp, dws, [x3s, accs])(
            x0, rims0, up, back, slope1
        )
        grads = reduce_grads(dw1, dw2, n_dp)
    return state2[None], grads


def solution(mesh):
    in_specs = (
        P("dp", "space", None, None, None),
        P(None, None, None, "dp", None),
        P("dp", "space", None, None, None),
        P("space", None, None),
    )
    out_specs = (P("dp", "space", None, None, None), P(None, None, None, "dp", None))
    body = functools.partial(per_device, mesh.shape["dp"], mesh.shape["space"])
    return jax.shard_map(
        body, mesh=mesh, in_specs=in_specs, out_specs=out_specs, check_vma=False
    )
```

```python
import functools

import jax
import jax.numpy as jnp
from jax import lax
from jax.experimental import pallas as pl
from jax.experimental.pallas import tpu as pltpu
from jax.sharding import PartitionSpec as P

LAYERS = 2
F32 = jnp.float32
BF16 = jnp.bfloat16


def edge_strips(field):
    return jnp.stack(
        [field[:, 0], field[:, -1], field[:, :, 0], field[:, :, -1]], axis=1
    )


def orient(strips, adjacency):
    selected = strips[adjacency[:, :, 0], adjacency[:, :, 1]]
    flipped = (adjacency[:, :, 2] == 1)[:, :, None, None]
    return jnp.where(flipped, selected[:, :, ::-1], selected)


def exchange(strips, adjacency):
    return orient(lax.all_gather(strips, "space", axis=0, tiled=True), adjacency)


def fill(x3, field, rims):
    s, _, c = field.shape
    col = lax.broadcasted_iota(jnp.int32, (s, s, c), 1)
    wide = field.astype(F32)
    if rims is None:
        left = right = jnp.zeros((1, 1, 1), F32)
    else:
        left = rims[2].astype(F32)[:, None, :]
        right = rims[3].astype(F32)[:, None, :]
    x3[1 : s + 1, :, c : 2 * c] = field
    x3[1 : s + 1, :, 0:c] = jnp.where(col == 0, left, pltpu.roll(wide, 1, 1)).astype(BF16)
    x3[1 : s + 1, :, 2 * c :] = jnp.where(
        col == s - 1, right, pltpu.roll(wide, s - 1, 1)
    ).astype(BF16)
    rc = lax.broadcasted_iota(jnp.int32, (s, c), 0)
    for row, edge in ((0, 0), (s + 1, 1)):
        if rims is None:
            x3[row] = jnp.zeros((s, 3 * c), BF16)
        else:
            line = rims[edge].astype(F32)
            x3[row, :, c : 2 * c] = rims[edge]
            x3[row, :, 0:c] = jnp.where(rc == 0, 0.0, pltpu.roll(line, 1, 0)).astype(BF16)
            x3[row, :, 2 * c :] = jnp.where(
                rc == s - 1, 0.0, pltpu.roll(line, s - 1, 0)
            ).astype(BF16)


def conv(x3, w):
    s = x3.shape[1]
    k = x3.shape[2]
    total = None
    for p in range(3):
        part = jnp.dot(
            x3[p : p + s].reshape(s * s, k), w[p], preferred_element_type=F32
        )
        total = part if total is None else total + part
    return total.reshape(s, s, -1)


def wgrad_add(acc, x3, grad):
    s = x3.shape[1]
    k = x3.shape[2]
    flipped = grad.reshape(s * s, -1).T
    for p in range(3):
        acc[p] += jnp.dot(
            flipped, x3[p : p + s].reshape(s * s, k), preferred_element_type=F32
        )


def k_first_send(x, rims, w, adj, state, slope, rims_out, x3, gath, sems):
    stream_begin()
    t = rims_out.shape[0]
    out = k_first(x, rims, w, state, slope, x3)
    put_strips(gath, t, pl.program_id(0), out)
    stream_tile(gath, sems, t, adj, rims_out)


def k_first_only(*refs):
    k_first(*refs)


def turn_weights(w, wt):
    c = w.shape[2]
    for p in range(3):
        for q in range(3):
            tap = w[2 - p, (2 - q) * c : (3 - q) * c]
            wt[p, q * c : (q + 1) * c] = tap.astype(F32).T.astype(BF16)


def k_last_send(
    x, rims, w, cot, adj, state, grad, back, dw, x3, g3, rim_grad, wt, held, acc, gath, sems
):
    t = back.shape[0]
    i = pl.program_id(0)
    stream_begin()

    @pl.when(i == 0)
    def _():
        turn_weights(w, wt)
        acc[...] = jnp.zeros_like(acc)

    fill(x3, x[0], rims[0])

    @pl.when(i < t)
    def _():
        k_last(x, rims, w, wt, cot, state, grad, rim_grad, x3, g3, False)
        held[i] = grad[0]
        me = lax.axis_index("space")
        base = (me * t + i) * 4
        for e in range(4):
            gath[base + e] = rim_grad[0, e]

    stream_tile(gath, sems, t, adj, back, True)

    @pl.when(i >= t)
    def _():
        wgrad_add(acc, x3, held[i - t])

    finish_wgrad(acc, dw)


def k_tail_send(
    n_dp, x, rims, g, w, cot, back, slope, dw2, dw, out, x3, g3, wt, acc, *sums
):
    i = pl.program_id(0)
    last = pl.num_programs(0) - 1
    peers, stages = sum_stages(n_dp, dw2, out, *sums)

    @pl.when(i == 0)
    def _():
        greet(peers)
        stages[0]()
        turn_weights(w, wt)
        acc[...] = jnp.zeros_like(acc)

    for step, stage in ((2, stages[1]), (4, stages[2]), (5, stages[3])):
        pl.when(i == jnp.minimum(step, last))(stage)
    fill(g3, g[0], None)
    tail_tile(x, rims, cot[0].astype(F32) + conv(g3, wt), back, slope, x3, acc)
    finish_wgrad(acc, dw)

    @pl.when(i == last)
    def _():
        stages[4]()
        stages[5]()


def k_first(x, rims, w, state, slope, x3):
    fill(x3, x[0], rims[0])
    v = conv(x3, w)
    sg = jax.nn.sigmoid(v)
    out = x[0].astype(F32) + v * sg
    state[0] = out.astype(BF16)
    slope[0] = (sg * (1.0 + v * (1.0 - sg))).astype(slope.dtype)
    return out


def k_last(x, rims, w, wt, cot, state, grad, rim_grad, x3, g3, build=True):
    s = x.shape[1]
    c = x.shape[3]
    if build:
        fill(x3, x[0], rims[0])
    v = conv(x3, w)
    sg = jax.nn.sigmoid(v)
    state[0] = (x[0].astype(F32) + v * sg).astype(BF16)
    g32 = cot[0].astype(F32) * (sg * (1.0 + v * (1.0 - sg)))
    g = g32.astype(BF16)
    grad[0] = g
    fill(g3, g, None)
    rim_grad[0, 0] = jnp.dot(g3[1], wt[2], preferred_element_type=F32).astype(BF16)
    rim_grad[0, 1] = jnp.dot(g3[s], wt[0], preferred_element_type=F32).astype(BF16)
    for edge, col, q in ((2, 0, 2), (3, s - 1, 0)):
        line = jnp.concatenate(
            [g3[p : p + s, :, c : 2 * c].astype(F32)[:, col, :] for p in range(3)], axis=1
        ).astype(BF16)
        weight = jnp.concatenate([wt[p, q * c : (q + 1) * c] for p in range(3)], axis=0)
        rim_grad[0, edge] = jnp.dot(line, weight, preferred_element_type=F32).astype(BF16)


def finish_wgrad(acc, out):
    @pl.when(pl.program_id(0) == pl.num_programs(0) - 1)
    def _():
        n, _, c = out.shape
        depth = c // n
        for p in range(3):
            for q in range(3):
                tap = acc[p, :, q * c : (q + 1) * c].T.astype(out.dtype)
                first = (3 * p + q) * depth
                out[:, first : first + depth, :] = tap.reshape(n, depth, c)


def k_back(x, rims, g, wt, cot, up, dw, x3, g3, acc):
    @pl.when(pl.program_id(0) == 0)
    def _():
        acc[...] = jnp.zeros_like(acc)

    fill(x3, x[0], rims[0])
    wgrad_add(acc, x3, g[0])
    fill(g3, g[0], None)
    up[0] = cot[0].astype(F32) + conv(g3, wt)
    finish_wgrad(acc, dw)


def tail_tile(x, rims, u, back, slope, x3, acc):
    s = x.shape[1]
    fill(x3, x[0], rims[0])
    row = lax.broadcasted_iota(jnp.int32, u.shape, 0)
    col = lax.broadcasted_iota(jnp.int32, u.shape, 1)
    r = back[0].astype(F32)
    u = u + jnp.where(row == 0, r[0][None], 0.0) + jnp.where(row == s - 1, r[1][None], 0.0)
    u = u + jnp.where(col == 0, r[2][:, None, :], 0.0)
    u = u + jnp.where(col == s - 1, r[3][:, None, :], 0.0)
    g = (u * slope[0].astype(F32)).astype(BF16)
    wgrad_add(acc, x3, g)


def k_tail(x, rims, up, back, slope, dw, x3, acc):
    @pl.when(pl.program_id(0) == 0)
    def _():
        acc[...] = jnp.zeros_like(acc)

    tail_tile(x, rims, up[0], back, slope, x3, acc)
    finish_wgrad(acc, dw)


def reduce_grads(dw1, dw2, n_dp):
    both = jnp.concatenate([dw1, dw2], axis=1)
    n, rows, c = both.shape
    part = lax.psum_scatter(both.astype(F32), "dp", scatter_dimension=0, tiled=True)
    return lax.psum(part, "space").reshape(LAYERS, 3, 3, c // n, c)


def remote(src, dst, sems, i, who):
    return pltpu.make_async_remote_copy(
        src_ref=src,
        dst_ref=dst,
        send_sem=sems.at[0, i],
        recv_sem=sems.at[1, i],
        device_id=who,
        device_id_type=pl.DeviceIdType.MESH,
    )


def square():
    me = lax.axis_index("space")
    xn = me + 1 - 2 * (me % 2)
    yn = (me + 2) % 4
    return me, xn, yn, (xn + 2) % 4


def seg(gath, t, dev, first, count):
    return gath.at[pl.ds((dev * t + first) * 4, 4 * count)]


def send_tiles(gath, sems, t, first, count, i):
    me, xn, yn, _ = square()
    mine = seg(gath, t, me, first, count)
    remote(mine, mine, sems, i, {"space": xn}).start()
    remote(mine, mine, sems, t + i, {"space": yn}).start()


def relay_tiles(gath, sems, t, first, count, i, by_x):
    _, xn, yn, _ = square()
    source, target = (xn, yn) if by_x else (yn, xn)
    got = seg(gath, t, source, first, count)
    remote(got, got, sems, i if by_x else t + i, {"space": source}).wait_recv()
    remote(got, got, sems, 2 * t + i, {"space": target}).start()


def drain_tiles(gath, sems, t, first, count, i, by_x):
    me, xn, yn, dg = square()
    mine = seg(gath, t, me, first, count)
    remote(mine, mine, sems, i, {"space": xn}).wait_send()
    remote(mine, mine, sems, t + i, {"space": yn}).wait_send()
    source, other = (xn, yn) if by_x else (yn, xn)
    got = seg(gath, t, source, first, count)
    remote(got, got, sems, 2 * t + i, {"space": other}).wait_send()
    late = seg(gath, t, other, first, count)
    remote(late, late, sems, t + i if by_x else i, {"space": other}).wait_recv()
    far = seg(gath, t, dg, first, count)
    remote(far, far, sems, 2 * t + i, {"space": other}).wait_recv()


def put_strips(gath, t, i, field):
    me = lax.axis_index("space")
    base = (me * t + i) * 4
    s = field.shape[0]
    gath[base] = field[0].astype(BF16)
    gath[base + 1] = field[s - 1].astype(BF16)
    gath[base + 2] = field[:, 0, :].astype(BF16)
    gath[base + 3] = field[:, s - 1, :].astype(BF16)


def orient_tiles(gath, adj, out):
    t = out.shape[0]
    s = out.shape[2]
    r = lax.broadcasted_iota(jnp.int32, (s, s), 0)
    c = lax.broadcasted_iota(jnp.int32, (s, s), 1)
    turn = jnp.where(r + c == s - 1, 1.0, 0.0).astype(BF16)

    def body(a, carry):
        for e in range(4):
            line = gath[adj[a, e, 0] * 4 + adj[a, e, 1]]
            back = jnp.dot(turn, line, preferred_element_type=F32)
            out[a, e] = jnp.where(adj[a, e, 2] == 1, back, line.astype(F32)).astype(BF16)
        return carry

    lax.fori_loop(0, t, body, 0)


def stream_begin():
    _, xn, yn, _ = square()

    @pl.when(pl.program_id(0) == 0)
    def _():
        greet([{"space": xn}, {"space": yn}])


def stream_tile(gath, sems, t, adj, out, phases=False):
    i = pl.program_id(0)
    h = t // 2

    def relay(j):
        pl.when(j < h)(lambda: relay_tiles(gath, sems, t, j, 1, j, True))
        pl.when(j >= h)(lambda: relay_tiles(gath, sems, t, j, 1, j, False))

    @pl.when(i < t)
    def _():
        send_tiles(gath, sems, t, i, 1, i)

    if phases:
        pl.when(jnp.logical_and(i > 1, i < t + 2))(lambda: relay(i - 2))
    else:
        pl.when(i > 0)(lambda: relay(i - 1))

    @pl.when(i == pl.num_programs(0) - 1)
    def _():
        if not phases:
            relay(i)
        for j in range(t):
            drain_tiles(gath, sems, t, j, 1, j, j < h)
        orient_tiles(gath, adj, out)


def greet(peers):
    barrier = pltpu.get_barrier_semaphore()
    for who in peers:
        pl.semaphore_signal(
            barrier, inc=1, device_id=who, device_id_type=pl.DeviceIdType.MESH
        )
    pl.semaphore_wait(barrier, len(peers))


def c_open(n_dp, w_in, x, adj, w_out, out, gath, sems, own, zs, ps):
    me, xn, yn, _ = square()
    line = n_dp // 2
    dp = lax.axis_index("dp")
    q, core = dp // 2, dp % 2
    depth = w_in.shape[3]
    layers = w_in.shape[0]
    right = {"dp": ((q + 1) % line) * 2 + core}
    left = {"dp": ((q + line - 1) % line) * 2 + core}
    partner = {"dp": q * 2 + 1 - core}
    greet([{"space": xn}, {"space": yn}, right, left, partner])
    t = x.shape[0]
    h = t // 2
    parts = ((0, h, True), (h, t - h, False))

    def build(a, carry):
        put_strips(gath, t, a, x[a].astype(F32))
        return carry

    def slot(l, o, c):
        return w_out.at[l, :, :, pl.ds(pl.multiple_of((o * 2 + c) * depth, depth), depth), :]

    keep = pltpu.make_async_copy(
        w_in, w_out.at[:, :, :, pl.ds(pl.multiple_of(dp * depth, depth), depth), :], own
    )
    keep.start()

    def move(l, o, who, sm, i, first):
        ref = w_in.at[l] if first else slot(l, o, core)
        return remote(ref, slot(l, o, core), sm, i, who)

    def zi(l, s, way):
        return (l * line + s) * 2 + way

    def forward(l, s, way, o, first):
        who = right if way == 0 else left
        ok = (q + 1 < line) if way == 0 else (q > 0)

        @pl.when(ok)
        def _():
            move(l, o, who, zs, zi(l, s, way), first).start()

    for l in range(layers):
        forward(l, 0, 0, q, True)
        forward(l, 0, 1, q, True)
        move(l, q, partner, ps, zi(l, 0, 0), True).start()
    lax.fori_loop(0, t, build, 0)
    for i, (first, count, _) in enumerate(parts):
        send_tiles(gath, sems, t, first, count, i)
    for l in range(layers):
        if l == 1:
            for i, (first, count, by_x) in enumerate(parts):
                relay_tiles(gath, sems, t, first, count, i, by_x)
        for s in range(1, line):
            for way in (0, 1):
                o = q - s if way == 0 else q + s
                ok = (o >= 0) if way == 0 else (o < line)

                @pl.when(ok)
                def _(l=l, s=s, way=way, o=o):
                    move(l, o, right, zs, zi(l, s - 1, way), False).wait_recv()
                    move(l, o, partner, ps, zi(l, s, way), False).start()
                    if s < line - 1:
                        forward(l, s, way, o, False)

    for l in range(layers):
        for s in range(line):
            for way in (0, 1):
                o = q - s if way == 0 else q + s
                ok = (o >= 0) if way == 0 else (o < line)
                if s == 0 and way == 1:
                    ok = None

                def part(l=l, s=s, way=way, o=o):
                    copy = move(l, o, partner, ps, zi(l, s, way), False)
                    copy.wait_send()
                    remote(
                        slot(l, o, 1 - core), slot(l, o, 1 - core), ps, zi(l, s, way), partner
                    ).wait_recv()

                if ok is not None:
                    pl.when(ok)(part)
                if s < line - 1:
                    sent = (
                        jnp.logical_and(o >= 0, q + 1 < line)
                        if way == 0
                        else jnp.logical_and(o < line, q > 0)
                    )

                    @pl.when(sent)
                    def _(l=l, s=s, way=way, o=o):
                        move(l, o, right, zs, zi(l, s, way), False).wait_send()

    for i, (first, count, by_x) in enumerate(parts):
        drain_tiles(gath, sems, t, first, count, i, by_x)
    keep.wait()
    orient_tiles(gath, adj, out)


def sum_stages(
    n_dp, g, out, b1, x_out, x_in, keep2, y_out, y_in, keep3, z_out, z_in, a_out, a_in, sems
):
    me, xn, yn, _ = square()
    line = n_dp // 2
    dp = lax.axis_index("dp")
    q, core = dp // 2, dp % 2
    rows = g.shape[2]
    rh = rows // 2
    ry = y_in.shape[1]
    partner = {"dp": q * 2 + 1 - core}
    zp = [{"dp": ((q + d) % line) * 2 + core} for d in range(1, line)]
    mx, my = me % 2, me // 2
    x_mine = pl.multiple_of(mx * rh, 16)
    x_give = pl.multiple_of((1 - mx) * rh, 16)
    y_mine = pl.multiple_of(my * (rh - ry), 16)
    y_give = pl.multiple_of((1 - my) * (rh - ry), 16)
    peers = [{"space": xn}, {"space": yn}, partner] + zp

    def half(first, i):
        return remote(
            g.at[:, 1 - core, pl.ds(first, rh)], b1.at[:, pl.ds(first, rh)], sems, i, partner
        )

    give = lambda: half(x_give, 0)
    have = lambda: half(x_mine, 1)
    sx = lambda: remote(x_out, x_in, sems, 2, {"space": xn})
    sy = lambda: remote(y_out, y_in, sems, 3, {"space": yn})
    sz = lambda d: remote(z_out.at[(q + d) % line], z_in.at[d - 1], sems, 3 + d, zp[d - 1])
    fy = lambda: remote(a_out, a_in.at[0], sems, 3 + line, {"space": yn})
    fx = lambda: remote(a_out, a_in.at[1], sems, 4 + line, {"space": xn})
    fz = lambda: remote(a_in.at[0], a_in.at[2], sems, 5 + line, {"space": xn})

    def s0():
        give().start()
        have().start()

    def s1():
        give().wait_recv()
        for l in range(line):
            x_out[l] = (
                g[l, core, pl.ds(x_give, rh)].astype(F32) + b1[l, pl.ds(x_give, rh)].astype(F32)
            ).astype(BF16)
        sx().start()
        have().wait_recv()
        for l in range(line):
            keep2[l] = g[l, core, pl.ds(x_mine, rh)].astype(F32) + b1[
                l, pl.ds(x_mine, rh)
            ].astype(F32)

    def s2():
        sx().wait_recv()
        for l in range(line):
            y_out[l] = (
                keep2[l, pl.ds(y_give, ry)] + x_in[l, pl.ds(y_give, ry)].astype(F32)
            ).astype(BF16)
        sy().start()
        for l in range(line):
            keep3[l] = keep2[l, pl.ds(y_mine, ry)] + x_in[l, pl.ds(y_mine, ry)].astype(F32)

    def s3():
        sy().wait_recv()
        for l in range(line):
            keep3[l] = keep3[l] + y_in[l].astype(F32)
        z_out[...] = keep3[...].astype(BF16)
        for d in range(1, line):
            sz(d).start()

    def s4():
        total = keep3[q]
        for d in range(1, line):
            sz(d).wait_recv()
            total = total + z_in[d - 1].astype(F32)
        a_out[...] = total.astype(BF16)
        fy().start()
        fx().start()

    def s5():
        fy().wait_recv()
        fz().start()
        out[pl.ds(pl.multiple_of(x_mine + y_mine, 16), ry)] = a_out[...].astype(F32)
        out[pl.ds(pl.multiple_of(x_mine + y_give, 16), ry)] = a_in[0].astype(F32)
        fx().wait_recv()
        out[pl.ds(pl.multiple_of(x_give + y_mine, 16), ry)] = a_in[1].astype(F32)
        fz().wait_recv()
        out[pl.ds(pl.multiple_of(x_give + y_give, 16), ry)] = a_in[2].astype(F32)
        for copy in [give, have, sx, sy, fy, fx, fz]:
            copy().wait_send()
        for d in range(1, line):
            sz(d).wait_send()

    return peers, [s0, s1, s2, s3, s4, s5]


def c_sum(n_dp, *refs):
    peers, stages = sum_stages(n_dp, *refs)
    greet(peers)
    for stage in stages:
        stage()


def sum_scratch(n_dp, rows, c):
    line = n_dp // 2
    rh = rows // 2
    ry = -(-(rh // 2) // 16) * 16
    vm = pltpu.VMEM
    return [
        vm((line, rows, c), BF16),
        vm((line, rh, c), BF16),
        vm((line, rh, c), BF16),
        vm((line, rh, c), F32),
        vm((line, ry, c), BF16),
        vm((line, ry, c), BF16),
        vm((line, ry, c), F32),
        vm((line, ry, c), BF16),
        vm((line - 1, ry, c), BF16),
        vm((ry, c), BF16),
        vm((3, ry, c), BF16),
        pltpu.SemaphoreType.DMA((2, 6 + line)),
    ]


VM = pl.BlockSpec(memory_space=pltpu.VMEM)


def params(cid):
    return pltpu.CompilerParams(
        collective_id=cid, has_side_effects=True, vmem_limit_bytes=60 << 20
    )


def open_gather(n_dp, kernels, x, adjacency):
    dma = pltpu.SemaphoreType.DMA
    shape = kernels.shape
    whole = shape[:3] + (shape[3] * n_dp, shape[4])
    return pl.pallas_call(
        functools.partial(c_open, n_dp),
        out_shape=(
            jax.ShapeDtypeStruct(whole, kernels.dtype),
            jax.ShapeDtypeStruct((x.shape[0], 4) + x.shape[2:], x.dtype),
        ),
        in_specs=[VM, VM, pl.BlockSpec(memory_space=pltpu.SMEM)],
        out_specs=(VM, VM),
        scratch_shapes=[
            pltpu.VMEM((16 * x.shape[0],) + x.shape[2:], x.dtype),
            dma((2, 3 * x.shape[0])),
            dma,
            dma((2, 2 * n_dp)),
            dma((2, 2 * n_dp)),
        ],
        compiler_params=params(0),
    )(kernels, x, adjacency)


def sum_grads(n_dp, g, cid):
    line = n_dp // 2
    rows, c = g.shape[1:]
    return pl.pallas_call(
        functools.partial(c_sum, n_dp),
        out_shape=jax.ShapeDtypeStruct((rows, c), F32),
        in_specs=[VM],
        out_specs=VM,
        scratch_shapes=sum_scratch(n_dp, rows, c),
        compiler_params=params(cid),
    )(g.reshape(line, 2, rows, c))


def per_device(n_dp, n_sp, inputs, kernels, cotangent, adjacency):
    _, t, s, _, c = inputs.shape
    x0 = inputs[0]
    cot = cotangent[0]
    if n_sp == 4:
        weights, rims0 = open_gather(n_dp, kernels, x0, adjacency)
    else:
        weights = lax.all_gather(kernels, "dp", axis=3, tiled=True)
        rims0 = exchange(edge_strips(x0), adjacency)
    w1 = weights[0].reshape(3, 3 * c, c)
    w2 = weights[1].reshape(3, 3 * c, c)
    wt = jnp.transpose(weights[1][::-1, ::-1], (0, 1, 3, 2)).reshape(3, 3 * c, c)

    tile = pl.BlockSpec((1, s, s, c), lambda i: (i, 0, 0, 0))
    rim = pl.BlockSpec((1, 4, s, c), lambda i: (i, 0, 0, 0))
    wsp = pl.BlockSpec((3, 3 * c, c), lambda i: (0, 0, 0), pipeline_mode=pl.Buffered(1))
    field = lambda dt: jax.ShapeDtypeStruct((t, s, s, c), dt)
    dws = jax.ShapeDtypeStruct((n_dp, 9 * c // n_dp, c), BF16)
    dwsp = pl.BlockSpec(dws.shape, lambda i: (0, 0, 0))
    x3s = pltpu.VMEM((s + 2, s, 3 * c), BF16)
    accs = pltpu.VMEM((3, c, 3 * c), F32)
    flops = 2 * t * s * s * c * c * 9
    plain = pltpu.CompilerParams(vmem_limit_bytes=60 << 20)
    call = lambda body, nf, ins, outs, shapes, scratch, extra=plain, steps=t: pl.pallas_call(
        body,
        grid=(steps,),
        in_specs=ins,
        out_specs=outs,
        out_shape=shapes,
        scratch_shapes=scratch,
        compiler_params=extra,
        cost_estimate=pl.CostEstimate(
            flops=nf * flops, bytes_accessed=12 << 20, transcendentals=0
        ),
    )
    rims = jax.ShapeDtypeStruct((t, 4, s, c), BF16)
    if n_sp == 4:
        smem = pl.BlockSpec(memory_space=pltpu.SMEM)
        whole = pl.BlockSpec((t, 4, s, c), lambda i: (0, 0, 0, 0))
        passing = [
            pltpu.VMEM((16 * t, s, c), BF16),
            pltpu.SemaphoreType.DMA((2, 3 * t)),
        ]
        state1, slope1, rims1 = call(
            k_first_send,
            1,
            [tile, rim, wsp, smem],
            [tile, tile, whole],
            [field(BF16), field(F32), rims],
            [x3s] + passing,
            params(1),
        )(x0, rims0, w1, adjacency)
        twice = pl.BlockSpec((1, s, s, c), lambda i: (i % t, 0, 0, 0))
        rim2 = pl.BlockSpec((1, 4, s, c), lambda i: (i % t, 0, 0, 0))
        once = pl.BlockSpec((1, s, s, c), lambda i: (jnp.minimum(i, t - 1), 0, 0, 0))
        wts = pltpu.VMEM((3, 3 * c, c), BF16)
        state2, g2, back, dw2 = call(
            k_last_send,
            2,
            [twice, rim2, wsp, once, smem],
            [once, once, whole, dwsp],
            [field(BF16), field(BF16), rims, dws],
            [x3s, x3s, pltpu.VMEM((1, 4, s, c), BF16), wts, pltpu.VMEM((t, s, s, c), BF16), accs]
            + passing,
            params(2),
            2 * t,
        )(state1, rims1, w2, cot, adjacency)
        rows = dws.shape[1]
        line = n_dp // 2
        wide = pl.BlockSpec((line, 2, rows, c), lambda i: (0, 0, 0, 0))
        flat = pl.BlockSpec((rows, c), lambda i: (0, 0))
        total = jax.ShapeDtypeStruct((rows, c), F32)
        dw1, sum2 = call(
            functools.partial(k_tail_send, n_dp),
            2,
            [tile, rim, tile, wsp, tile, rim, tile, wide],
            [dwsp, flat],
            [dws, total],
            [x3s, x3s, wts, accs] + sum_scratch(n_dp, rows, c),
            params(4),
        )(x0, rims0, g2, w2, cot, back, slope1, dw2.reshape(line, 2, rows, c))
        sum1 = sum_grads(n_dp, dw1, 3)
        grads = jnp.stack([sum1, sum2]).reshape(LAYERS, 3, 3, c // n_dp, c)
    else:
        state1, slope1 = call(
            k_first_only, 1, [tile, rim, wsp], [tile, tile], [field(BF16), field(F32)], [x3s]
        )(x0, rims0, w1)
        rims1 = exchange(edge_strips(state1), adjacency)
        state2, g2, rg = call(
            k_last,
            1,
            [tile, rim, wsp, wsp, tile],
            [tile, tile, rim],
            [field(BF16), field(BF16), rims],
            [x3s, x3s],
        )(state1, rims1, w2, wt, cot)
        back = exchange(rg, adjacency)
        up, dw2 = call(
            k_back,
            2,
            [tile, rim, tile, wsp, tile],
            [tile, dwsp],
            [field(F32), dws],
            [x3s, x3s, accs],
        )(state1, rims1, g2, wt, cot)
        dw1 = call(k_tail, 1, [tile, rim, tile, rim, tile], dwsp, dws, [x3s, accs])(
            x0, rims0, up, back, slope1
        )
        grads = reduce_grads(dw1, dw2, n_dp)
    return state2[None], grads


def solution(mesh):
    in_specs = (
        P("dp", "space", None, None, None),
        P(None, None, None, "dp", None),
        P("dp", "space", None, None, None),
        P("space", None, None),
    )
    out_specs = (P("dp", "space", None, None, None), P(None, None, None, "dp", None))
    body = functools.partial(per_device, mesh.shape["dp"], mesh.shape["space"])
    return jax.shard_map(
        body, mesh=mesh, in_specs=in_specs, out_specs=out_specs, check_vma=False
    )
```
